32 devices in a mesh: row: 4 (over y, x), col: 8 (over z, core).
Axes of the slice: x: 2, y: 2, z: 4, core: 2. Of those that a mesh axis runs over, the one named last changes fastest.
Arguments:
- tokens: bfloat16 [128, 512, 192], P('row', 'col'), may hold values from -6 to 6
- norm_gain: float32 [2, 3, 192], replicated, may hold values from 0.1 to 1.9
- qkv_weight: bfloat16 [2, 192, 576], replicated, may hold values from -0.4375 to 0.4375
- proj_weight: bfloat16 [2, 192, 192], replicated, may hold values from -0.4375 to 0.4375
- bias_table: float32 [2, 6, 225], replicated, may hold values from -4 to 4
- conv_weight: float32 [2, 49, 192], replicated, may hold values from -0.875 to 0.875
- up_weight: bfloat16 [2, 192, 768], replicated, may hold values from -0.4375 to 0.4375
- down_weight: bfloat16 [2, 768, 192], replicated, may hold values from -0.21875 to 0.21875
Outputs:
- mixed: bfloat16 [128, 512, 192], P('row', 'col')
The draws below stay inside these ranges and needn't reach their ends.
All inputs are finite; a program needn't handle non-finite values.
Results may differ from the reference program's by a relative error of at most 0.013.
Values may be sent and summed in bfloat16 or wider, within the bound.
A program may use at most 64 MiB of HBM per device.

```python
import math
import jax
import jax.numpy as jnp
from jax import lax

D = 192
HEADS = 6
HID = 768
WS = 8
KS = 7
LAYERS = 2
HEAD = 32
ROWS = 128
COLS = 512


def block_scale(key, dims, split, low, high):
    loudness = 1.0
    for dim, shards_of in split:
        steps = jax.random.uniform(jax.random.fold_in(jax.random.fold_in(key, 6), dim), (shards_of,), jnp.float32, low / len(split), high / len(split))
        loudness = loudness * jnp.repeat(jnp.exp(steps), dims[dim] // shards_of).reshape((-1,) + (1,) * (len(dims) - 1 - dim))
    return loudness


def scatter_about(stream_key, dims, scale, bound, pieces=(), held_as=jnp.bfloat16):
    factor_of = block_scale(stream_key, dims, pieces, -0.22, 0.18) if pieces else 1.0
    values = jax.random.normal(stream_key, dims, jnp.float32) * scale * factor_of
    return jnp.minimum(jnp.maximum(values, -bound), bound).astype(held_as)


def setup_inputs(seed: int = 0) -> dict:
    streams_of = jax.random.split(jax.random.key(seed), 9)
    return {
        "tokens": scatter_about(streams_of[0], (ROWS, COLS, D), 1.0, 6.0, ((0, 4), (1, 8))),
        "norm_gain": jnp.clip(1.0 + 0.18 * jax.random.normal(streams_of[1], (LAYERS, 3, D), jnp.float32), 0.1, 1.9),
        "qkv_weight": scatter_about(streams_of[2], (LAYERS, D, 3 * D), D ** -0.5, 0.4375),
        "proj_weight": scatter_about(streams_of[3], (LAYERS, D, D), D ** -0.5, 0.4375),
        "bias_table": scatter_about(streams_of[4], (LAYERS, HEADS, (2 * WS - 1) * (2 * WS - 1)), 1.0, 4.0, (), jnp.float32),
        "conv_weight": scatter_about(streams_of[5], (LAYERS, KS * KS, D), (KS * KS) ** -0.5, 0.875, (), jnp.float32),
        "up_weight": scatter_about(streams_of[6], (LAYERS, D, HID), D ** -0.5, 0.4375),
        "down_weight": scatter_about(streams_of[7], (LAYERS, HID, D), HID ** -0.5, 0.21875),
    }


epsilon = 1e-05

def layer_norm(values, scaling):
    values = values.astype(jnp.float32)
    centre = lax.optimization_barrier(jnp.mean(values, axis=-1, keepdims=True))
    centred = values - centre
    spread = lax.optimization_barrier(jnp.mean(centred * centred, axis=-1, keepdims=True))
    return (centred * lax.rsqrt(spread + epsilon) * scaling).astype(jnp.bfloat16)

def position_bias(lookup_table):
    window_area = WS * WS
    places = jnp.arange(window_area, dtype=jnp.int32)
    place_row = places // WS
    place_col = places % WS
    offsets = (place_row[:, None] - place_row[None, :] + WS - 1) * (2 * WS - 1) + (place_col[:, None] - place_col[None, :] + WS - 1)
    entries = jnp.arange((2 * WS - 1) * (2 * WS - 1), dtype=jnp.int32)
    selector = (offsets.reshape(-1)[:, None] == entries[None, :]).astype(jnp.float32)
    expanded = jnp.dot(selector, lookup_table.T, precision=lax.Precision.HIGHEST)
    return expanded.reshape(window_area, window_area, HEADS).transpose(2, 0, 1)

def window_attention(windows, qkv_matrix, proj_matrix, score_bias):
    window_count = windows.shape[0]
    projected = jnp.dot(windows.reshape(-1, D), qkv_matrix, preferred_element_type=jnp.float32)
    projected = projected.astype(jnp.bfloat16).reshape(window_count, WS * WS, 3, HEADS, HEAD)
    query = projected[:, :, 0].astype(jnp.float32)
    keys_all = projected[:, :, 1].astype(jnp.float32)
    value_all = projected[:, :, 2].astype(jnp.float32)
    scores = jnp.einsum('wqhd,wkhd->whqk', query, keys_all, precision=lax.Precision.HIGHEST)
    scores = scores * HEAD ** (-0.5) + score_bias[None]
    weights = jnp.exp(scores)
    attention_weights = (weights / lax.optimization_barrier(jnp.sum(weights, axis=-1, keepdims=True))).astype(jnp.bfloat16)
    attended = jnp.einsum('whqk,wkhd->wqhd', attention_weights.astype(jnp.float32), value_all, precision=lax.Precision.HIGHEST)
    attended = attended.astype(jnp.bfloat16).reshape(window_count * WS * WS, D)
    branch = jnp.dot(attended, proj_matrix, preferred_element_type=jnp.float32).astype(jnp.bfloat16)
    return branch.reshape(window_count, WS * WS, D)

def shuffle_windows(token_grid):
    height, width = (token_grid.shape[0], token_grid.shape[1])
    return token_grid.reshape(WS, height // WS, WS, width // WS, D).transpose(1, 3, 0, 2, 4).reshape(-1, WS * WS, D)

def shuffle_back(windows, height, width):
    return windows.reshape(height // WS, width // WS, WS, WS, D).transpose(2, 0, 3, 1, 4).reshape(height, width, D)

def plain_windows(token_grid):
    height, width = (token_grid.shape[0], token_grid.shape[1])
    return token_grid.reshape(height // WS, WS, width // WS, WS, D).transpose(0, 2, 1, 3, 4).reshape(-1, WS * WS, D)

def plain_back(windows, height, width):
    return windows.reshape(height // WS, width // WS, WS, WS, D).transpose(0, 2, 1, 3, 4).reshape(height, width, D)

def depthwise(padded, kernel, height, width):
    accumulated = jnp.zeros((height, width, D), jnp.float32)
    for tap_row in range(KS):
        for tap_col in range(KS):
            accumulated = accumulated + padded[tap_row:tap_row + height, tap_col:tap_col + width].astype(jnp.float32) * kernel[tap_row * KS + tap_col]
    return accumulated

def feed_forward(normed, up_matrix, down_matrix):
    hidden = jax.nn.gelu(jnp.dot(normed, up_matrix, preferred_element_type=jnp.float32), approximate=False).astype(jnp.bfloat16)
    return jnp.dot(hidden, down_matrix, preferred_element_type=jnp.float32)

def reference(tokens, norm_gain, qkv_weight, proj_weight, bias_table, conv_weight, up_weight, down_weight):
    height, width = (tokens.shape[0], tokens.shape[1])
    halo_width = KS // 2
    current = tokens
    for layer_index in range(LAYERS):
        normed = layer_norm(current, norm_gain[layer_index, 0])
        if layer_index % 2 == 1:
            windows = shuffle_windows(normed)
        else:
            windows = plain_windows(normed)
        score_bias = position_bias(bias_table[layer_index])
        window_count = windows.shape[0]
        group_size = math.gcd(window_count, 256)
        qkv_matrix = qkv_weight[layer_index]
        proj_matrix = proj_weight[layer_index]
        attended = lax.map(lambda window_block: window_attention(window_block, qkv_matrix, proj_matrix, score_bias), windows.reshape(window_count // group_size, group_size, WS * WS, D))
        attended = attended.reshape(window_count, WS * WS, D)
        if layer_index % 2 == 1:
            branch = shuffle_back(attended, height, width)
        else:
            branch = plain_back(attended, height, width)
        after_attention = current.astype(jnp.float32) + branch.astype(jnp.float32)
        normed_two = layer_norm(after_attention, norm_gain[layer_index, 1])
        padded = jnp.pad(normed_two, ((halo_width, halo_width), (halo_width, halo_width), (0, 0)))
        after_conv = after_attention + depthwise(padded, conv_weight[layer_index], height, width)
        stripe_rows = math.gcd(height, 16)
        gain_three = norm_gain[layer_index, 2]
        up_matrix = up_weight[layer_index]
        down_matrix = down_weight[layer_index]

        def finish(rows_in):
            flat_rows = rows_in.reshape(-1, D)
            normed_three = layer_norm(flat_rows, gain_three)
            return (flat_rows + feed_forward(normed_three, up_matrix, down_matrix)).astype(jnp.bfloat16).reshape(rows_in.shape)
        current = lax.map(finish, after_conv.reshape(height // stripe_rows, stripe_rows, width, D)).reshape(height, width, D)
    return current
```

```python
import functools

import jax
import jax.numpy as jnp
from jax import lax
from jax.experimental import pallas as pl
from jax.experimental.pallas import tpu as pltpu
from jax.sharding import PartitionSpec as P

D = 192
HEADS = 6
WS = 8
KS = 7
LAYERS = 2
HEAD = 32
AREA = WS * WS
HALO = KS // 2

epsilon = 1e-05
LOG2E = 1.4426950408889634
VALUE_SCALE = 2.0**-8
EXP_CAP = 3.3895313892515355e38


def padded_2(cells, sides, width):
    for axis, dim in sides:
        count = lax.axis_size(axis)
        ends = count - 1
        head = lax.slice_in_dim(cells, 0, width, axis=dim)
        tail = lax.slice_in_dim(cells, cells.shape[dim] - width, cells.shape[dim], axis=dim)
        cells = jnp.concatenate(
            [
                lax.ppermute(tail, axis, [(i, (i + 1) % count) for i in range(ends)]),
                cells,
                lax.ppermute(head, axis, [((i + 1) % count, i) for i in range(ends)]),
            ],
            axis=dim,
        )
    return cells


def norm(values, gain):
    centre = jnp.mean(values, axis=-1, keepdims=True)
    centred = values - centre
    spread = jnp.mean(centred * centred, axis=-1, keepdims=True)
    return centred * lax.rsqrt(spread + epsilon) * gain


def score_bias(lookup_table):
    places = jnp.arange(AREA, dtype=jnp.int32)
    row, col = places // WS, places % WS
    offsets = (row[:, None] - row[None, :] + WS - 1) * (2 * WS - 1) + (
        col[:, None] - col[None, :] + WS - 1
    )
    entries = jnp.arange((2 * WS - 1) * (2 * WS - 1), dtype=jnp.int32)
    selector = (offsets.reshape(-1)[:, None] == entries[None, :]).astype(jnp.float32)
    expanded = jnp.dot(lookup_table, selector.T, precision=lax.Precision.HIGHEST) * LOG2E
    return expanded.reshape(HEADS, AREA, AREA).transpose(1, 0, 2).reshape(AREA, HEADS * AREA)


def attention(normed, qkv_ref, proj_ref, bias_ref):
    count = normed.shape[0] // AREA
    query, key, value = (
        jnp.dot(normed, qkv_ref[part], preferred_element_type=jnp.float32).astype(jnp.bfloat16)
        for part in range(3)
    )
    lane_head = lax.broadcasted_iota(jnp.int32, (1, D), 1) // HEAD
    masks = [(lane_head == head).astype(jnp.bfloat16) for head in range(HEADS)]
    value_masks = [mask * VALUE_SCALE for mask in masks]
    sums = jnp.concatenate([jnp.broadcast_to(mask, (AREA, D)) for mask in value_masks], axis=0)
    bias = bias_ref[...]
    outs, exps = [], []
    for window in range(count):
        rows = slice(window * AREA, (window + 1) * AREA)
        keys = jnp.concatenate([key[rows] * mask for mask in masks], axis=0)
        scores = lax.dot_general(
            query[rows], keys, (((1,), (1,)), ((), ())), preferred_element_type=jnp.float32
        )
        exped = jnp.minimum(jnp.exp2(scores * (HEAD**-0.5 * LOG2E) + bias), EXP_CAP)
        exped = exped.astype(jnp.bfloat16)
        values = jnp.concatenate([value[rows] * mask for mask in value_masks], axis=0)
        outs.append(jnp.dot(exped, values, preferred_element_type=jnp.float32))
        exps.append(exped)
    total = jnp.dot(jnp.concatenate(exps, axis=0), sums, preferred_element_type=jnp.float32)
    attended = (jnp.concatenate(outs, axis=0) / total).astype(jnp.bfloat16)
    branch = jnp.dot(attended, proj_ref[...], preferred_element_type=jnp.float32)
    return branch.astype(jnp.bfloat16).astype(jnp.float32)


def regular_kernel(x_ref, gain_ref, qkv_ref, proj_ref, bias_ref, after_ref, normed_ref):
    rows, width = x_ref.shape[0], x_ref.shape[1]
    current = x_ref[...].astype(jnp.float32)
    normed = norm(current.reshape(rows * width, D), gain_ref[0])
    windows = normed.reshape(WS, width // WS, WS, D).transpose(1, 0, 2, 3).reshape(rows * width, D)
    branch = attention(windows.astype(jnp.bfloat16), qkv_ref, proj_ref, bias_ref)
    branch = branch.reshape(width // WS, WS, WS, D).transpose(1, 0, 2, 3).reshape(rows, width, D)
    after = current + branch
    after_ref[...] = after
    normed_ref[...] = norm(after, gain_ref[1]).astype(jnp.bfloat16)


def shuffle_kernel(x_ref, qkv_ref, proj_ref, bias_ref, out_ref):
    across = x_ref.shape[3]
    tokens = x_ref[:, 0].astype(jnp.float32)
    windows = jnp.swapaxes(tokens, 1, 2).transpose(1, 0, 2, 3).reshape(across * AREA, D)
    branch = attention(windows.astype(jnp.bfloat16), qkv_ref, proj_ref, bias_ref)
    branch = branch.reshape(across, WS, WS, D).transpose(1, 0, 2, 3)
    out_ref[:, 0] = jnp.swapaxes(branch, 1, 2).astype(jnp.bfloat16)


def residual_kernel(x_ref, branch_ref, gain_ref, after_ref, normed_ref):
    after = x_ref[...].astype(jnp.float32) + branch_ref[...].astype(jnp.float32)
    after_ref[...] = after
    normed_ref[...] = norm(after, gain_ref[1]).astype(jnp.bfloat16)


def conv_mlp_kernel(
    padded_ref, after_ref, gain_ref, taps_ref, up_ref, down_ref, *rest
):
    out_refs, (wide, taps, conv) = rest[:-3], rest[-3:]
    rows, width = after_ref.shape[0], after_ref.shape[1]
    step = pl.program_id(0)

    @pl.when(step == 0)
    def _():
        wide[:, : padded_ref.shape[1], :] = padded_ref[...].astype(jnp.float32)
        taps[...] = jnp.broadcast_to(taps_ref[...][:, None, :], taps.shape)

    base = step * rows
    for left in range(0, width, 8):
        for lanes in (slice(0, 128), slice(128, D)):
            sums = [after_ref[r, left : left + 8, lanes] for r in range(rows)]
            for v in range(KS):
                weights = [taps[u * KS + v, :, lanes] for u in range(KS)]
                for r in range(rows + KS - 1):
                    cell = wide[base + r, left + v : left + v + 8, lanes]
                    for u in range(KS):
                        if 0 <= r - u < rows:
                            sums[r - u] = sums[r - u] + cell * weights[u]
            for r in range(rows):
                conv[r, left : left + 8, lanes] = sums[r]
    flat = conv[...].reshape(rows * width, D)
    normed = norm(flat, gain_ref[2]).astype(jnp.bfloat16)
    up = jnp.dot(normed, up_ref[...], preferred_element_type=jnp.float32)
    hidden = (0.5 * up * (1.0 + lax.erf(up * 0.5**0.5))).astype(jnp.bfloat16)
    outcome = flat + jnp.dot(hidden, down_ref[...], preferred_element_type=jnp.float32)
    current = outcome.astype(jnp.bfloat16)
    out_refs[0][...] = current.reshape(rows, width, D)
    if len(out_refs) == 2:
        following = norm(current.astype(jnp.float32), gain_ref[3])
        out_refs[1][...] = following.astype(jnp.bfloat16).reshape(rows, width, D)


def whole(shape):
    return pl.BlockSpec(shape, lambda i: (0,) * len(shape))


def stripe(width):
    return pl.BlockSpec((WS, width, D), lambda i: (i, 0, 0))


def shuffled(normed, qkv, proj, bias):
    height, width = normed.shape[0], normed.shape[1]
    row_count, col_count = lax.axis_size("row"), lax.axis_size("col")
    row_repeat, col_repeat = max(1, WS // row_count), max(1, WS // col_count)
    row_piece = height // row_repeat // row_count
    col_piece = width // col_repeat // col_count
    layout = normed.reshape(row_repeat, row_count, row_piece, col_repeat, col_count, col_piece, D)
    outgoing = layout.transpose(1, 4, 0, 2, 3, 5, 6).reshape(
        row_count * col_count, row_repeat, row_piece, col_repeat, col_piece, D
    )
    received = lax.all_to_all(outgoing, ("row", "col"), split_axis=0, concat_axis=0, tiled=True)
    grid = received.reshape(
        row_count, col_count, row_repeat, row_piece, col_repeat, col_piece, D
    ).transpose(0, 2, 3, 1, 4, 5, 6)
    down = row_count * row_repeat * row_piece // WS
    across = col_count * col_repeat * col_piece // WS
    grid = grid.reshape(WS, down, WS, across, D)
    block = pl.BlockSpec((WS, 1, WS, across, D), lambda i: (0, i, 0, 0, 0))
    result = pl.pallas_call(
        shuffle_kernel,
        out_shape=jax.ShapeDtypeStruct(grid.shape, jnp.bfloat16),
        grid=(down,),
        in_specs=[block, whole(qkv.shape), whole(proj.shape), whole(bias.shape)],
        out_specs=block,
        name="shuffle_attention",
    )(grid, qkv, proj, bias)
    result = result.reshape(
        row_count, row_repeat, row_piece, col_count, col_repeat, col_piece, D
    ).transpose(0, 3, 1, 2, 4, 5, 6)
    result = result.reshape(row_count * col_count, row_repeat, row_piece, col_repeat, col_piece, D)
    returned = lax.all_to_all(result, ("row", "col"), split_axis=0, concat_axis=0, tiled=True)
    returned = returned.reshape(
        row_count, col_count, row_repeat, row_piece, col_repeat, col_piece, D
    ).transpose(2, 0, 3, 4, 1, 5, 6)
    return returned.reshape(height, width, D)


def on_device(
    tokens, norm_gain, qkv_weight, proj_weight, bias_table, conv_weight, up_weight, down_weight
):
    height, width = tokens.shape[0], tokens.shape[1]
    shape32 = jax.ShapeDtypeStruct(tokens.shape, jnp.float32)
    shape16 = jax.ShapeDtypeStruct(tokens.shape, jnp.bfloat16)
    qkv_parts = qkv_weight.reshape(LAYERS, D, 3, D).transpose(0, 2, 1, 3)
    current, normed = tokens, None
    for layer in range(LAYERS):
        bias = score_bias(bias_table[layer])
        gains = norm_gain[layer][:, None, :]
        qkv, proj = qkv_parts[layer], proj_weight[layer]
        if layer % 2 == 0:
            after, normed_two = pl.pallas_call(
                regular_kernel,
                out_shape=(shape32, shape16),
                grid=(height // WS,),
                in_specs=[
                    stripe(width),
                    whole(gains.shape),
                    whole(qkv.shape),
                    whole(proj.shape),
                    whole(bias.shape),
                ],
                out_specs=(stripe(width), stripe(width)),
                name="regular_attention",
            )(current, gains, qkv, proj, bias)
        else:
            branch = shuffled(normed, qkv, proj, bias)
            after, normed_two = pl.pallas_call(
                residual_kernel,
                out_shape=(shape32, shape16),
                grid=(height // WS,),
                in_specs=[stripe(width), stripe(width), whole(gains.shape)],
                out_specs=(stripe(width), stripe(width)),
                name="residual",
            )(current, branch, gains)
        padded = padded_2(normed_two, (("row", 0), ("col", 1)), HALO)
        last = layer == LAYERS - 1
        if not last:
            gains = jnp.concatenate([gains, norm_gain[layer + 1, :1][:, None, :]], axis=0)
        outs = pl.pallas_call(
            conv_mlp_kernel,
            out_shape=(shape16,) if last else (shape16, shape16),
            grid=(height // WS,),
            in_specs=[
                whole(padded.shape),
                stripe(width),
                whole(gains.shape),
                whole((KS * KS, D)),
                whole(up_weight.shape[1:]),
                whole(down_weight.shape[1:]),
            ],
            out_specs=(stripe(width),) if last else (stripe(width), stripe(width)),
            scratch_shapes=[
                pltpu.VMEM((padded.shape[0], -(-padded.shape[1] // 8) * 8, D), jnp.float32),
                pltpu.VMEM((KS * KS, 8, D), jnp.float32),
                pltpu.VMEM((WS, width, D), jnp.float32),
            ],
            name="conv_mlp",
        )(padded, after, gains, conv_weight[layer], up_weight[layer], down_weight[layer])
        current = outs[0]
        normed = None if last else outs[1]
    return current


def solution(mesh):
    in_specs = (P("row", "col", None), P(), P(), P(), P(), P(), P(), P())
    return jax.shard_map(
        on_device, mesh=mesh, in_specs=in_specs, out_specs=P("row", "col", None), check_vma=False
    )
```

```python
import functools

import jax
import jax.numpy as jnp
from jax import lax
from jax.experimental import pallas as pl
from jax.experimental.pallas import tpu as pltpu
from jax.sharding import PartitionSpec as P

D = 192
HEADS = 6
WS = 8
KS = 7
LAYERS = 2
HEAD = 32
AREA = WS * WS
HALO = KS // 2

epsilon = 1e-05
LOG2E = 1.4426950408889634
VALUE_SCALE = 2.0**-8
EXP_CAP = 3.3895313892515355e38
MESH = pl.DeviceIdType.MESH
SIDES = [(d, a) for d in (-1, 0, 1) for a in (-1, 0, 1) if d or a]


def norm(values, gain):
    centre = jnp.mean(values, axis=-1, keepdims=True)
    centred = values - centre
    spread = jnp.mean(centred * centred, axis=-1, keepdims=True)
    return centred * lax.rsqrt(spread + epsilon) * gain


def score_bias(lookup_table):
    places = jnp.arange(AREA, dtype=jnp.int32)
    row, col = places // WS, places % WS
    offsets = (row[:, None] - row[None, :] + WS - 1) * (2 * WS - 1) + (
        col[:, None] - col[None, :] + WS - 1
    )
    entries = jnp.arange((2 * WS - 1) * (2 * WS - 1), dtype=jnp.int32)
    selector = (offsets.reshape(-1)[:, None] == entries[None, :]).astype(jnp.float32)
    expanded = jnp.dot(lookup_table, selector.T, precision=lax.Precision.HIGHEST) * LOG2E
    return expanded.reshape(HEADS, AREA, AREA).transpose(1, 0, 2).reshape(AREA, HEADS * AREA)


def attention(normed, qkv_ref, proj_ref, bias_ref):
    count = normed.shape[0] // AREA
    query, key, value = (
        jnp.dot(normed, qkv_ref[part], preferred_element_type=jnp.float32).astype(jnp.bfloat16)
        for part in range(3)
    )
    lane_head = lax.broadcasted_iota(jnp.int32, (1, D), 1) // HEAD
    masks = [(lane_head == head).astype(jnp.bfloat16) for head in range(HEADS)]
    value_masks = [mask * VALUE_SCALE for mask in masks]
    sums = jnp.concatenate([jnp.broadcast_to(mask, (AREA, D)) for mask in value_masks], axis=0)
    bias = bias_ref[...]
    outs, exps = [], []
    for window in range(count):
        rows = slice(window * AREA, (window + 1) * AREA)
        keys = jnp.concatenate([key[rows] * mask for mask in masks], axis=0)
        scores = lax.dot_general(
            query[rows], keys, (((1,), (1,)), ((), ())), preferred_element_type=jnp.float32
        )
        exped = jnp.minimum(jnp.exp2(scores * (HEAD**-0.5 * LOG2E) + bias), EXP_CAP)
        exped = exped.astype(jnp.bfloat16)
        values = jnp.concatenate([value[rows] * mask for mask in value_masks], axis=0)
        outs.append(jnp.dot(exped, values, preferred_element_type=jnp.float32))
        exps.append(exped)
    total = jnp.dot(jnp.concatenate(exps, axis=0), sums, preferred_element_type=jnp.float32)
    attended = (jnp.concatenate(outs, axis=0) / total).astype(jnp.bfloat16)
    branch = jnp.dot(attended, proj_ref[...], preferred_element_type=jnp.float32)
    return branch.astype(jnp.bfloat16).astype(jnp.float32)


def regular_kernel(x_ref, gain_ref, qkv_ref, proj_ref, bias_ref, after_ref, normed_ref):
    rows, width = x_ref.shape[0], x_ref.shape[1]
    current = x_ref[...].astype(jnp.float32)
    normed = norm(current.reshape(rows * width, D), gain_ref[0])
    windows = normed.reshape(WS, width // WS, WS, D).transpose(1, 0, 2, 3).reshape(rows * width, D)
    branch = attention(windows.astype(jnp.bfloat16), qkv_ref, proj_ref, bias_ref)
    branch = branch.reshape(width // WS, WS, WS, D).transpose(1, 0, 2, 3).reshape(rows, width, D)
    after = current + branch
    after_ref[...] = after
    normed_ref[...] = norm(after, gain_ref[1]).astype(jnp.bfloat16)


def greet(everyone):
    rows, cols = lax.axis_size("row"), lax.axis_size("col")
    my_row, my_col = lax.axis_index("row"), lax.axis_index("col")
    barrier = pltpu.get_barrier_semaphore()
    if everyone:

        @pl.loop(0, rows * cols)
        def _(device):
            row, col = device // cols, device % cols

            @pl.when((row != my_row) | (col != my_col))
            def _():
                pl.semaphore_signal(barrier, 1, device_id=(row, col), device_id_type=MESH)

        pl.semaphore_wait(barrier, rows * cols - 1)
    else:
        for down, across in SIDES:
            row, col = my_row + down, my_col + across
            inside = (row >= 0) & (row < rows) & (col >= 0) & (col < cols)

            @pl.when(inside)
            def _():
                pl.semaphore_signal(barrier, 1, device_id=(row, col), device_id_type=MESH)

        beside_rows = (my_row > 0).astype(jnp.int32) + (my_row < rows - 1).astype(jnp.int32)
        beside_cols = (my_col > 0).astype(jnp.int32) + (my_col < cols - 1).astype(jnp.int32)
        pl.semaphore_wait(barrier, (1 + beside_rows) * (1 + beside_cols) - 1)


def exchange(normed_ref, wide, beside, above, corner, send_sem, recv_sem):
    rows, cols = lax.axis_size("row"), lax.axis_size("col")
    my_row, my_col = lax.axis_index("row"), lax.axis_index("col")
    height, blocks = normed_ref.shape[0], normed_ref.shape[1]
    width = blocks * 8
    links = []
    for number, (down, across) in enumerate(SIDES):
        row, col = my_row + down, my_col + across
        there = (row >= 0) & (row < rows) & (col >= 0) & (col < cols)
        back_row, back_col = my_row - down, my_col - across
        here = (back_row >= 0) & (back_row < rows) & (back_col >= 0) & (back_col < cols)
        picked = {-1: slice(0, HALO), 0: slice(0, height), 1: slice(height - HALO, height)}[down]
        if across == 0:
            source, target = normed_ref.at[picked], above.at[(1 - down) // 2]
        else:
            block = 0 if across < 0 else blocks - 1
            source = normed_ref.at[picked, block]
            side = (1 - across) // 2
            target = beside.at[side] if down == 0 else corner.at[(1 - down) // 2, side]
        copy = pltpu.make_async_remote_copy(
            source,
            target,
            send_sem.at[number],
            recv_sem.at[number],
            device_id=(row, col),
            device_id_type=MESH,
        )
        links.append((down, across, there, here, copy))
        pl.when(there)(copy.start)

    @pl.loop(0, height)
    def _(r):
        wide[HALO + r, 8 : 8 + width, :] = normed_ref[r].astype(jnp.float32).reshape(width, D)

    for down, across, there, here, copy in links:
        rows_at = {1: slice(0, HALO), 0: slice(HALO, HALO + height), -1: slice(HALO + height, None)}
        cols_at = {1: slice(0, 8), 0: slice(8, 8 + width), -1: slice(8 + width, None)}
        at = (rows_at[down], cols_at[across])

        @pl.when(here)
        def _():
            copy.wait_recv()
            if across == 0:
                landed = above[(1 - down) // 2].astype(jnp.float32).reshape(HALO, width, D)
            elif down == 0:
                landed = beside[(1 - across) // 2].astype(jnp.float32)
            else:
                landed = corner[(1 - down) // 2, (1 - across) // 2].astype(jnp.float32)
            wide[at[0], at[1], :] = landed

        @pl.when(jnp.logical_not(here))
        def _():
            wide[at[0], at[1], :] = jnp.zeros_like(wide[at[0], at[1], :])

        pl.when(there)(copy.wait_send)


def mix(base, after, wide, taps, conv, gain_ref, up_ref, down_ref):
    rows, width = after.shape[0], after.shape[1]

    for left in range(0, width, 8):
        for lanes in (slice(0, 128), slice(128, D)):
            sums = after[:, left : left + 8, lanes]
            for v in range(KS):
                start = left + 8 - HALO + v
                cells = wide[pl.ds(base, rows + KS - 1), start : start + 8, lanes]
                for u in range(KS):
                    sums = sums + cells[u : u + rows] * taps[u * KS + v, :, lanes][None]
            conv[:, left : left + 8, lanes] = sums

    flat = conv[...].reshape(rows * width, D)
    normed = norm(flat, gain_ref[2]).astype(jnp.bfloat16)
    up = jnp.dot(normed, up_ref[...], preferred_element_type=jnp.float32)
    hidden = (0.5 * up * (1.0 + lax.erf(up * 0.5**0.5))).astype(jnp.bfloat16)
    outcome = flat + jnp.dot(hidden, down_ref[...], preferred_element_type=jnp.float32)
    return outcome.astype(jnp.bfloat16)


def first_mix_kernel(
    normed_ref,
    after_ref,
    gain_ref,
    taps_ref,
    up_ref,
    down_ref,
    out_ref,
    received,
    wide,
    taps,
    conv,
    beside,
    above,
    corner,
    halo_send,
    halo_recv,
    outgoing,
    send_sem,
    recv_sem,
):
    rows, width = after_ref.shape[0], after_ref.shape[1]
    row_count, col_count, row_repeat, pairs, col_piece = received.shape[:5]
    per_step = rows // (2 * pairs)
    my_row, my_col = lax.axis_index("row"), lax.axis_index("col")
    step = pl.program_id(0)

    @pl.when(step == 0)
    def _():
        greet(True)
        taps[...] = jnp.broadcast_to(taps_ref[...][:, None, :], taps.shape)
        exchange(normed_ref, wide, beside, above, corner, halo_send, halo_recv)

    current = mix(step * rows, after_ref, wide, taps, conv, gain_ref, up_ref, down_ref)
    out_ref[...] = current.reshape(rows, width, D)
    following = norm(current.astype(jnp.float32), gain_ref[3]).reshape(rows, width, D)

    for k in range(per_step):
        for pair in range(pairs):
            row = (k * pairs + pair) * 2
            packed = jnp.concatenate([following[row], following[row + 1]], axis=-1)
            for col in range(col_count):
                piece = packed[col * col_piece : (col + 1) * col_piece]
                outgoing[step * per_step + k, col, pair] = piece.astype(jnp.bfloat16)

    def remote(chunk, col):
        return pltpu.make_async_remote_copy(
            outgoing.at[chunk, col],
            received.at[my_row, my_col, chunk // row_count],
            send_sem.at[chunk, col],
            recv_sem.at[my_row, my_col, chunk // row_count],
            device_id=(chunk % row_count, col),
            device_id_type=MESH,
        )

    for k in range(per_step):
        chunk = step * per_step + k

        @pl.loop(0, col_count)
        def _(turn):
            col = (my_col + turn) % col_count
            mine = (chunk % row_count == my_row) & (col == my_col)

            @pl.when(mine)
            def _():
                pltpu.make_async_copy(
                    outgoing.at[chunk, col],
                    received.at[my_row, my_col, chunk // row_count],
                    recv_sem.at[my_row, my_col, chunk // row_count],
                ).start()

            @pl.when(jnp.logical_not(mine))
            def _():
                remote(chunk, col).start()

    @pl.when(step == pl.num_programs(0) - 1)
    def _():
        @pl.loop(0, row_count * row_repeat)
        def _(chunk):
            @pl.loop(0, col_count)
            def _(col):
                mine = (chunk % row_count == my_row) & (col == my_col)

                @pl.when(jnp.logical_not(mine))
                def _():
                    remote(chunk, col).wait_send()

                row, repeat = chunk % row_count, chunk // row_count
                pltpu.make_async_copy(
                    outgoing.at[chunk, col],
                    received.at[row, col, repeat],
                    recv_sem.at[row, col, repeat],
                ).wait()


def shuffle_kernel(
    x_ref, qkv_ref, proj_ref, bias_ref, returned, outgoing, send_sem, recv_sem
):
    row_count, col_count, row_repeat, pairs, col_piece = returned.shape[:5]
    per_b = col_count // WS
    across = per_b * col_piece
    my_row, my_col = lax.axis_index("row"), lax.axis_index("col")
    step = pl.program_id(0)

    @pl.when(step == 0)
    def _():
        greet(True)

    tokens = x_ref[:, :, :, 0].astype(jnp.float32).transpose(0, 2, 1, 3, 4)
    tokens = tokens.reshape(WS, WS, per_b, col_piece, 2 * D)
    if per_b == 1:
        tokens = tokens[:, :, 0]
    else:
        tokens = jnp.concatenate([tokens[:, :, part] for part in range(per_b)], axis=2)
    results = []
    for half in range(2):
        windows = jnp.swapaxes(tokens[..., half * D : (half + 1) * D], 1, 2)
        windows = windows.transpose(1, 0, 2, 3).reshape(across * AREA, D)
        branch = attention(windows.astype(jnp.bfloat16), qkv_ref, proj_ref, bias_ref)
        branch = branch.reshape(across, WS, WS, D).transpose(1, 0, 2, 3)
        results.append(jnp.swapaxes(branch, 1, 2))
    packed = jnp.concatenate(results, axis=-1).reshape(row_count, row_repeat, WS, across, 2 * D)
    for col in range(col_count):
        part = col % per_b
        piece = packed[:, :, col // per_b, part * col_piece : (part + 1) * col_piece]
        outgoing[step, :, col] = piece.astype(jnp.bfloat16)

    def remote(pair, row, col):
        return pltpu.make_async_remote_copy(
            outgoing.at[pair, row, col],
            returned.at[my_row, my_col, :, pair],
            send_sem.at[pair, row, col],
            recv_sem.at[pair, my_row, my_col],
            device_id=(row, col),
            device_id_type=MESH,
        )

    def local(pair, row, col):
        return pltpu.make_async_copy(
            outgoing.at[pair, row, col],
            returned.at[row, col, :, pair],
            recv_sem.at[pair, row, col],
        )

    @pl.loop(0, row_count)
    def _(row):
        @pl.loop(0, col_count)
        def _(turn):
            col = (my_col + turn) % col_count
            mine = (row == my_row) & (col == my_col)
            pl.when(mine)(lambda: local(step, row, col).start())
            pl.when(jnp.logical_not(mine))(lambda: remote(step, row, col).start())

    @pl.when(step == pl.num_programs(0) - 1)
    def _():
        @pl.loop(0, row_count * pairs)
        def _(both):
            pair, row = both // row_count, both % row_count

            @pl.loop(0, col_count)
            def _(col):
                mine = (row == my_row) & (col == my_col)
                pl.when(jnp.logical_not(mine))(lambda: remote(pair, row, col).wait_send())
                local(pair, row, col).wait()


def last_mix_kernel(
    current_ref,
    returned_ref,
    gain_ref,
    taps_ref,
    up_ref,
    down_ref,
    out_ref,
    after,
    normed,
    wide,
    taps,
    conv,
    beside,
    above,
    corner,
    halo_send,
    halo_recv,
):
    rows, width = out_ref.shape[0], out_ref.shape[1]
    row_count, col_count, row_repeat, pairs, col_piece = returned_ref.shape[:5]
    step = pl.program_id(0)

    @pl.when(step == 0)
    def _():
        taps[...] = jnp.broadcast_to(taps_ref[...][:, None, :], taps.shape)

        @pl.loop(0, row_count * row_repeat)
        def _(chunk):
            for pair in range(pairs):
                packed = returned_ref[chunk % row_count, :, chunk // row_count, pair]
                packed = packed.astype(jnp.float32).reshape(width, 2 * D)
                for half in range(2):
                    row = (chunk * pairs + pair) * 2 + half
                    total = current_ref[row].astype(jnp.float32)
                    total = total + packed[:, half * D : (half + 1) * D]
                    after[row] = total
                    normed[row] = (
                        norm(total, gain_ref[1]).reshape(width // 8, 8, D).astype(jnp.bfloat16)
                    )

        greet(False)
        exchange(normed, wide, beside, above, corner, halo_send, halo_recv)

    base = step * rows
    current = mix(
        base, after.at[pl.ds(base, rows)], wide, taps, conv, gain_ref, up_ref, down_ref
    )
    out_ref[...] = current.reshape(rows, width, D)


def whole(shape):
    return pl.BlockSpec(shape, lambda i: (0,) * len(shape))


def stripe(width):
    return pl.BlockSpec((WS, width, D), lambda i: (i, 0, 0))


def mix_scratch(height, width):
    dma = pltpu.SemaphoreType.DMA
    return [
        pltpu.VMEM((height + 2 * HALO, width + 16, D), jnp.float32),
        pltpu.VMEM((KS * KS, 8, D), jnp.float32),
        pltpu.VMEM((WS, width, D), jnp.float32),
        pltpu.VMEM((2, height, 8, D), jnp.bfloat16),
        pltpu.VMEM((2, HALO, width // 8, 8, D), jnp.bfloat16),
        pltpu.VMEM((2, 2, HALO, 8, D), jnp.bfloat16),
        dma((len(SIDES),)),
        dma((len(SIDES),)),
    ]


def on_device(
    tokens, norm_gain, qkv_weight, proj_weight, bias_table, conv_weight, up_weight, down_weight
):
    height, width = tokens.shape[0], tokens.shape[1]
    row_count, col_count = lax.axis_size("row"), lax.axis_size("col")
    row_repeat = max(1, WS // row_count)
    row_piece = height // row_repeat // row_count
    col_piece = width // col_count
    pairs = row_piece // 2
    dma = pltpu.SemaphoreType.DMA
    shape32 = jax.ShapeDtypeStruct(tokens.shape, jnp.float32)
    shape16 = jax.ShapeDtypeStruct(tokens.shape, jnp.bfloat16)
    blocked = (height, width // 8, 8, D)
    moved = jax.ShapeDtypeStruct(
        (row_count, col_count, row_repeat, pairs, col_piece, 2 * D), jnp.bfloat16
    )
    qkv_parts = qkv_weight.reshape(LAYERS, D, 3, D).transpose(0, 2, 1, 3)
    biases = [score_bias(bias_table[layer]) for layer in range(LAYERS)]
    gains = jnp.concatenate([norm_gain, jnp.roll(norm_gain[:, :1], -1, axis=0)], axis=1)
    gains = gains[:, :, None, :]
    gain_shape = gains.shape[1:]
    weight_specs = [
        whole(gain_shape),
        whole((KS * KS, D)),
        whole(up_weight.shape[1:]),
        whole(down_weight.shape[1:]),
    ]
    attention_specs = [whole(qkv_parts.shape[1:]), whole((D, D)), whole(biases[0].shape)]

    after, normed_two = pl.pallas_call(
        regular_kernel,
        out_shape=(shape32, shape16),
        grid=(height // WS,),
        in_specs=[stripe(width), whole(gain_shape)] + attention_specs,
        out_specs=(stripe(width), stripe(width)),
        name="regular_attention",
    )(tokens, gains[0], qkv_parts[0], proj_weight[0], biases[0])

    current, received = pl.pallas_call(
        first_mix_kernel,
        out_shape=(shape16, moved),
        grid=(height // WS,),
        in_specs=[whole(blocked), stripe(width)] + weight_specs,
        out_specs=(stripe(width), pl.BlockSpec(memory_space=pl.ANY)),
        scratch_shapes=mix_scratch(height, width)
        + [
            pltpu.VMEM(
                (row_repeat * row_count, col_count, pairs, col_piece, 2 * D), jnp.bfloat16
            ),
            dma((row_repeat * row_count, col_count)),
            dma((row_count, col_count, row_repeat)),
        ],
        compiler_params=pltpu.CompilerParams(collective_id=0, has_side_effects=True),
        name="first_mix",
    )(
        normed_two.reshape(blocked),
        after,
        gains[0],
        conv_weight[0],
        up_weight[0],
        down_weight[0],
    )

    returned = pl.pallas_call(
        shuffle_kernel,
        out_shape=moved,
        grid=(pairs,),
        in_specs=[
            pl.BlockSpec(
                (row_count, col_count, row_repeat, 1, col_piece, 2 * D),
                lambda i: (0, 0, 0, i, 0, 0),
            )
        ]
        + attention_specs,
        out_specs=pl.BlockSpec(memory_space=pl.ANY),
        scratch_shapes=[
            pltpu.VMEM(
                (pairs, row_count, col_count, row_repeat, col_piece, 2 * D), jnp.bfloat16
            ),
            dma((pairs, row_count, col_count)),
            dma((pairs, row_count, col_count)),
        ],
        compiler_params=pltpu.CompilerParams(collective_id=1, has_side_effects=True),
        name="shuffle_attention",
    )(received, qkv_parts[1], proj_weight[1], biases[1])

    return pl.pallas_call(
        last_mix_kernel,
        out_shape=shape16,
        grid=(height // WS,),
        in_specs=[whole(tokens.shape), whole(moved.shape)] + weight_specs,
        out_specs=stripe(width),
        scratch_shapes=[
            pltpu.VMEM(tokens.shape, jnp.float32),
            pltpu.VMEM(blocked, jnp.bfloat16),
        ]
        + mix_scratch(height, width),
        compiler_params=pltpu.CompilerParams(collective_id=2, has_side_effects=True),
        name="last_mix",
    )(current, returned, gains[1], conv_weight[1], up_weight[1], down_weight[1])


def solution(mesh):
    in_specs = (P("row", "col", None), P(), P(), P(), P(), P(), P(), P())
    return jax.shard_map(
        on_device, mesh=mesh, in_specs=in_specs, out_specs=P("row", "col", None), check_vma=False
    )
```

```python
import functools

import jax
import jax.numpy as jnp
from jax import lax
from jax.experimental import pallas as pl
from jax.experimental.pallas import tpu as pltpu
from jax.sharding import PartitionSpec as P

D = 192
HEADS = 6
WS = 8
KS = 7
LAYERS = 2
HEAD = 32
AREA = WS * WS
HALO = KS // 2
LANES = 128

epsilon = 1e-05
LOG2E = 1.4426950408889634
VALUE_SCALE = 2.0**-8
EXP_CAP = 3.3895313892515355e38
MESH = pl.DeviceIdType.MESH
SIDES = [(d, a) for d in (-1, 0, 1) for a in (-1, 0, 1) if d or a]


def norm(values, gain):
    centre = jnp.mean(values, axis=-1, keepdims=True)
    centred = values - centre
    spread = jnp.mean(centred * centred, axis=-1, keepdims=True)
    return centred * lax.rsqrt(spread + epsilon) * gain


def score_biases(lookup_tables):
    places = jnp.arange(AREA, dtype=jnp.int32)
    row, col = places // WS, places % WS
    offsets = (row[:, None] - row[None, :] + WS - 1) * (2 * WS - 1) + (
        col[:, None] - col[None, :] + WS - 1
    )
    entries = jnp.arange((2 * WS - 1) * (2 * WS - 1), dtype=jnp.int32)
    selector = (offsets.reshape(-1)[None, :] == entries[:, None]).astype(jnp.float32)
    tables = lookup_tables.reshape(LAYERS * HEADS, -1)
    expanded = jnp.dot(tables, selector, precision=lax.Precision.HIGHEST) * LOG2E
    expanded = expanded.reshape(LAYERS, HEADS, AREA, AREA).transpose(0, 2, 1, 3)
    return expanded.reshape(LAYERS, AREA, HEADS * AREA)


def attention(normed, qkv_ref, proj_ref, bias_ref):
    count = normed.shape[0] // AREA
    query, key, value = (
        jnp.dot(
            normed, qkv_ref[:, part * D : (part + 1) * D], preferred_element_type=jnp.float32
        ).astype(jnp.bfloat16)
        for part in range(3)
    )
    lane_head = lax.broadcasted_iota(jnp.int32, (1, D), 1) // HEAD
    masks = [(lane_head == head).astype(jnp.bfloat16) for head in range(HEADS)]
    value_masks = [mask * VALUE_SCALE for mask in masks]
    sums = jnp.concatenate([jnp.broadcast_to(mask, (AREA, D)) for mask in value_masks], axis=0)
    bias = bias_ref[...]
    outs, exps = [], []
    for window in range(count):
        rows = slice(window * AREA, (window + 1) * AREA)
        keys = jnp.concatenate([key[rows] * mask for mask in masks], axis=0)
        scores = lax.dot_general(
            query[rows], keys, (((1,), (1,)), ((), ())), preferred_element_type=jnp.float32
        )
        exped = jnp.minimum(jnp.exp2(scores * (HEAD**-0.5 * LOG2E) + bias), EXP_CAP)
        exped = exped.astype(jnp.bfloat16)
        values = jnp.concatenate([value[rows] * mask for mask in value_masks], axis=0)
        outs.append(jnp.dot(exped, values, preferred_element_type=jnp.float32))
        exps.append(exped)
    total = jnp.dot(jnp.concatenate(exps, axis=0), sums, preferred_element_type=jnp.float32)
    attended = (jnp.concatenate(outs, axis=0) / total).astype(jnp.bfloat16)
    branch = jnp.dot(attended, proj_ref[...], preferred_element_type=jnp.float32)
    return branch.astype(jnp.bfloat16).astype(jnp.float32)


def regular_kernel(x_ref, gain_ref, qkv_ref, proj_ref, bias_ref, after_ref, normed_ref):
    rows, width = x_ref.shape[0], x_ref.shape[1]
    current = x_ref[...].astype(jnp.float32)
    normed = norm(current.reshape(rows * width, D), gain_ref[0, 0:1])
    windows = normed.reshape(WS, width // WS, WS, D).transpose(1, 0, 2, 3).reshape(rows * width, D)
    branch = attention(windows.astype(jnp.bfloat16), qkv_ref, proj_ref, bias_ref)
    branch = branch.reshape(width // WS, WS, WS, D).transpose(1, 0, 2, 3).reshape(rows, width, D)
    after = current + branch
    after_ref[...] = after
    normed_ref[...] = norm(after, gain_ref[0, 1:2]).astype(jnp.bfloat16)


def greet(everyone):
    rows, cols = lax.axis_size("row"), lax.axis_size("col")
    my_row, my_col = lax.axis_index("row"), lax.axis_index("col")
    barrier = pltpu.get_barrier_semaphore()
    if everyone:

        @pl.loop(0, rows * cols)
        def _(device):
            row, col = device // cols, device % cols

            @pl.when((row != my_row) | (col != my_col))
            def _():
                pl.semaphore_signal(barrier, 1, device_id=(row, col), device_id_type=MESH)

        pl.semaphore_wait(barrier, rows * cols - 1)
    else:
        for down, across in SIDES:
            row, col = my_row + down, my_col + across
            inside = (row >= 0) & (row < rows) & (col >= 0) & (col < cols)

            @pl.when(inside)
            def _():
                pl.semaphore_signal(barrier, 1, device_id=(row, col), device_id_type=MESH)

        beside_rows = (my_row > 0).astype(jnp.int32) + (my_row < rows - 1).astype(jnp.int32)
        beside_cols = (my_col > 0).astype(jnp.int32) + (my_col < cols - 1).astype(jnp.int32)
        pl.semaphore_wait(barrier, (1 + beside_rows) * (1 + beside_cols) - 1)


def exchange(normed_ref, wide, beside, above, corner, send_sem, recv_sem):
    rows, cols = lax.axis_size("row"), lax.axis_size("col")
    my_row, my_col = lax.axis_index("row"), lax.axis_index("col")
    height, blocks = normed_ref.shape[0], normed_ref.shape[1]
    width = blocks * 8
    links = []
    for number, (down, across) in enumerate(SIDES):
        row, col = my_row + down, my_col + across
        there = (row >= 0) & (row < rows) & (col >= 0) & (col < cols)
        back_row, back_col = my_row - down, my_col - across
        here = (back_row >= 0) & (back_row < rows) & (back_col >= 0) & (back_col < cols)
        picked = {-1: slice(0, HALO), 0: slice(0, height), 1: slice(height - HALO, height)}[down]
        if across == 0:
            source, target = normed_ref.at[picked], above.at[(1 - down) // 2]
        else:
            block = 0 if across < 0 else blocks - 1
            source = normed_ref.at[picked, block]
            side = (1 - across) // 2
            target = beside.at[side] if down == 0 else corner.at[(1 - down) // 2, side]
        copy = pltpu.make_async_remote_copy(
            source,
            target,
            send_sem.at[number],
            recv_sem.at[number],
            device_id=(row, col),
            device_id_type=MESH,
        )
        links.append((down, across, there, here, copy))
        pl.when(there)(copy.start)

    @pl.loop(0, height)
    def _(r):
        wide[HALO + r, 8 : 8 + width, :] = normed_ref[r].astype(jnp.float32).reshape(width, D)

    for down, across, there, here, copy in links:
        rows_at = {1: slice(0, HALO), 0: slice(HALO, HALO + height), -1: slice(HALO + height, None)}
        cols_at = {1: slice(0, 8), 0: slice(8, 8 + width), -1: slice(8 + width, None)}
        at = (rows_at[down], cols_at[across])

        @pl.when(here)
        def _():
            copy.wait_recv()
            if across == 0:
                landed = above[(1 - down) // 2].astype(jnp.float32).reshape(HALO, width, D)
            elif down == 0:
                landed = beside[(1 - across) // 2].astype(jnp.float32)
            else:
                landed = corner[(1 - down) // 2, (1 - across) // 2].astype(jnp.float32)
            wide[at[0], at[1], :] = landed

        @pl.when(jnp.logical_not(here))
        def _():
            wide[at[0], at[1], :] = jnp.zeros_like(wide[at[0], at[1], :])

        pl.when(there)(copy.wait_send)


def shift(wide, low, high, taps, taps_ref):
    width = low.shape[2]
    upper = taps_ref[:, LANES:]
    taps[0] = jnp.broadcast_to(taps_ref[:, :LANES][:, None, :], taps.shape[1:])
    both = jnp.concatenate([upper, upper], axis=-1)
    taps[1] = jnp.broadcast_to(both[:, None, :], taps.shape[1:])

    @pl.loop(0, wide.shape[0])
    def _(r):
        for v in range(KS):
            start = 8 - HALO + v
            low[v, r] = wide[r, start : start + width, :LANES]
            left = wide[r, start : start + width // 2, LANES:]
            right = wide[r, start + width // 2 : start + width, LANES:]
            high[v, r] = jnp.concatenate([left, right], axis=-1)


def mix(base, after, low, high, taps, conv, gain, up_ref, down_ref):
    rows, width = after.shape[0], after.shape[1]

    def tapped(cells, weights, left):
        sums = None
        for v in range(KS):
            for u in range(KS):
                term = cells[v, pl.ds(base + u, rows), left : left + 8, :]
                term = term * weights[u * KS + v][None]
                sums = term if sums is None else sums + term
        return sums

    for left in range(0, width, 8):
        at = slice(left, left + 8)
        conv[:, at, :LANES] = after[:, at, :LANES] + tapped(low, taps.at[0], left)
    for left in range(0, width // 2, 8):
        sums = tapped(high, taps.at[1], left)
        for half in range(2):
            at = slice(left + half * (width // 2), left + half * (width // 2) + 8)
            part = sums[:, :, half * (D - LANES) : (half + 1) * (D - LANES)]
            conv[:, at, LANES:] = after[:, at, LANES:] + part

    flat = conv[...].reshape(rows * width, D)
    normed = norm(flat, gain).astype(jnp.bfloat16)
    up = jnp.dot(normed, up_ref[...], preferred_element_type=jnp.float32)
    hidden = (0.5 * up * (1.0 + lax.erf(up * 0.5**0.5))).astype(jnp.bfloat16)
    outcome = flat + jnp.dot(hidden, down_ref[...], preferred_element_type=jnp.float32)
    return outcome.astype(jnp.bfloat16)


def first_mix_kernel(
    normed_ref,
    after_ref,
    gain_ref,
    taps_ref,
    up_ref,
    down_ref,
    out_ref,
    received,
    wide,
    low,
    high,
    taps,
    conv,
    beside,
    above,
    corner,
    halo_send,
    halo_recv,
    outgoing,
    send_sem,
    recv_sem,
):
    rows, width = after_ref.shape[0], after_ref.shape[1]
    row_count, col_count, row_repeat, pairs, col_piece = received.shape[:5]
    per_step = rows // (2 * pairs)
    my_row, my_col = lax.axis_index("row"), lax.axis_index("col")
    step = pl.program_id(0)

    @pl.when(step == 0)
    def _():
        greet(True)
        exchange(normed_ref, wide, beside, above, corner, halo_send, halo_recv)
        shift(wide, low, high, taps, taps_ref)

    gain = gain_ref[0, 2:3]
    current = mix(step * rows, after_ref, low, high, taps, conv, gain, up_ref, down_ref)
    out_ref[...] = current.reshape(rows, width, D)
    following = norm(current.astype(jnp.float32), gain_ref[1, 0:1]).reshape(rows, width, D)

    for k in range(per_step):
        for pair in range(pairs):
            row = (k * pairs + pair) * 2
            packed = jnp.concatenate([following[row], following[row + 1]], axis=-1)
            for col in range(col_count):
                piece = packed[col * col_piece : (col + 1) * col_piece]
                outgoing[step * per_step + k, col, pair] = piece.astype(jnp.bfloat16)

    def remote(chunk, col):
        return pltpu.make_async_remote_copy(
            outgoing.at[chunk, col],
            received.at[my_row, my_col, chunk // row_count],
            send_sem.at[chunk, col],
            recv_sem.at[my_row, my_col, chunk // row_count],
            device_id=(chunk % row_count, col),
            device_id_type=MESH,
        )

    for k in range(per_step):
        chunk = step * per_step + k

        @pl.loop(0, col_count)
        def _(turn):
            col = (my_col + turn) % col_count
            mine = (chunk % row_count == my_row) & (col == my_col)

            @pl.when(mine)
            def _():
                pltpu.make_async_copy(
                    outgoing.at[chunk, col],
                    received.at[my_row, my_col, chunk // row_count],
                    recv_sem.at[my_row, my_col, chunk // row_count],
                ).start()

            @pl.when(jnp.logical_not(mine))
            def _():
                remote(chunk, col).start()

    @pl.when(step == pl.num_programs(0) - 1)
    def _():
        @pl.loop(0, row_count * row_repeat)
        def _(chunk):
            @pl.loop(0, col_count)
            def _(col):
                mine = (chunk % row_count == my_row) & (col == my_col)

                @pl.when(jnp.logical_not(mine))
                def _():
                    remote(chunk, col).wait_send()

                row, repeat = chunk % row_count, chunk // row_count
                pltpu.make_async_copy(
                    outgoing.at[chunk, col],
                    received.at[row, col, repeat],
                    recv_sem.at[row, col, repeat],
                ).wait()


def shuffle_kernel(
    x_ref, qkv_ref, proj_ref, bias_ref, returned, outgoing, send_sem, recv_sem
):
    row_count, col_count, row_repeat, pairs, col_piece = returned.shape[:5]
    per_b = col_count // WS
    across = per_b * col_piece
    my_row, my_col = lax.axis_index("row"), lax.axis_index("col")
    step = pl.program_id(0)

    @pl.when(step == 0)
    def _():
        greet(True)

    tokens = x_ref[:, :, :, 0].astype(jnp.float32).transpose(0, 2, 1, 3, 4)
    tokens = tokens.reshape(WS, WS, per_b, col_piece, 2 * D)
    if per_b == 1:
        tokens = tokens[:, :, 0]
    else:
        tokens = jnp.concatenate([tokens[:, :, part] for part in range(per_b)], axis=2)
    results = []
    for half in range(2):
        windows = jnp.swapaxes(tokens[..., half * D : (half + 1) * D], 1, 2)
        windows = windows.transpose(1, 0, 2, 3).reshape(across * AREA, D)
        branch = attention(windows.astype(jnp.bfloat16), qkv_ref, proj_ref, bias_ref)
        branch = branch.reshape(across, WS, WS, D).transpose(1, 0, 2, 3)
        results.append(jnp.swapaxes(branch, 1, 2))
    packed = jnp.concatenate(results, axis=-1).reshape(row_count, row_repeat, WS, across, 2 * D)
    for col in range(col_count):
        part = col % per_b
        piece = packed[:, :, col // per_b, part * col_piece : (part + 1) * col_piece]
        outgoing[step, :, col] = piece.astype(jnp.bfloat16)

    def remote(pair, row, col):
        return pltpu.make_async_remote_copy(
            outgoing.at[pair, row, col],
            returned.at[my_row, my_col, :, pair],
            send_sem.at[pair, row, col],
            recv_sem.at[pair, my_row, my_col],
            device_id=(row, col),
            device_id_type=MESH,
        )

    def local(pair, row, col):
        return pltpu.make_async_copy(
            outgoing.at[pair, row, col],
            returned.at[row, col, :, pair],
            recv_sem.at[pair, row, col],
        )

    @pl.loop(0, row_count)
    def _(row):
        @pl.loop(0, col_count)
        def _(turn):
            col = (my_col + turn) % col_count
            mine = (row == my_row) & (col == my_col)
            pl.when(mine)(lambda: local(step, row, col).start())
            pl.when(jnp.logical_not(mine))(lambda: remote(step, row, col).start())

    @pl.when(step == pl.num_programs(0) - 1)
    def _():
        @pl.loop(0, row_count * pairs)
        def _(both):
            pair, row = both // row_count, both % row_count

            @pl.loop(0, col_count)
            def _(col):
                mine = (row == my_row) & (col == my_col)
                pl.when(jnp.logical_not(mine))(lambda: remote(pair, row, col).wait_send())
                local(pair, row, col).wait()


def last_mix_kernel(
    current_ref,
    returned_ref,
    gain_ref,
    taps_ref,
    up_ref,
    down_ref,
    out_ref,
    after,
    normed,
    wide,
    low,
    high,
    taps,
    conv,
    beside,
    above,
    corner,
    halo_send,
    halo_recv,
):
    rows, width = out_ref.shape[0], out_ref.shape[1]
    row_count, col_count, row_repeat, pairs, col_piece = returned_ref.shape[:5]
    step = pl.program_id(0)

    @pl.when(step == 0)
    def _():

        @pl.loop(0, row_count * row_repeat)
        def _(chunk):
            for pair in range(pairs):
                packed = returned_ref[chunk % row_count, :, chunk // row_count, pair]
                packed = packed.astype(jnp.float32).reshape(width, 2 * D)
                for half in range(2):
                    row = (chunk * pairs + pair) * 2 + half
                    total = current_ref[row].astype(jnp.float32)
                    total = total + packed[:, half * D : (half + 1) * D]
                    after[row] = total
                    normed[row] = (
                        norm(total, gain_ref[1, 1:2]).reshape(width // 8, 8, D).astype(jnp.bfloat16)
                    )

        greet(False)
        exchange(normed, wide, beside, above, corner, halo_send, halo_recv)
        shift(wide, low, high, taps, taps_ref)

    base = step * rows
    gain = gain_ref[1, 2:3]
    stripes = after.at[pl.ds(base, rows)]
    current = mix(base, stripes, low, high, taps, conv, gain, up_ref, down_ref)
    out_ref[...] = current.reshape(rows, width, D)


def whole(shape):
    return pl.BlockSpec(shape, lambda i: (0,) * len(shape))


def layer_of(array, layer):
    block = (None,) + array.shape[1:]
    return pl.BlockSpec(block, lambda i: (layer,) + (0,) * (len(block) - 1))


def stripe(width):
    return pl.BlockSpec((WS, width, D), lambda i: (i, 0, 0))


def mix_scratch(height, width):
    dma = pltpu.SemaphoreType.DMA
    return [
        pltpu.VMEM((height + 2 * HALO, width + 16, D), jnp.float32),
        pltpu.VMEM((KS, height + 2 * HALO, width, LANES), jnp.float32),
        pltpu.VMEM((KS, height + 2 * HALO, width // 2, LANES), jnp.float32),
        pltpu.VMEM((2, KS * KS, 8, LANES), jnp.float32),
        pltpu.VMEM((WS, width, D), jnp.float32),
        pltpu.VMEM((2, height, 8, D), jnp.bfloat16),
        pltpu.VMEM((2, HALO, width // 8, 8, D), jnp.bfloat16),
        pltpu.VMEM((2, 2, HALO, 8, D), jnp.bfloat16),
        dma((len(SIDES),)),
        dma((len(SIDES),)),
    ]


def on_device(
    tokens, norm_gain, qkv_weight, proj_weight, bias_table, conv_weight, up_weight, down_weight
):
    height, width = tokens.shape[0], tokens.shape[1]
    row_count, col_count = lax.axis_size("row"), lax.axis_size("col")
    row_repeat = max(1, WS // row_count)
    row_piece = height // row_repeat // row_count
    col_piece = width // col_count
    pairs = row_piece // 2
    dma = pltpu.SemaphoreType.DMA
    shape32 = jax.ShapeDtypeStruct(tokens.shape, jnp.float32)
    shape16 = jax.ShapeDtypeStruct(tokens.shape, jnp.bfloat16)
    blocked = (height, width // 8, 8, D)
    moved = jax.ShapeDtypeStruct(
        (row_count, col_count, row_repeat, pairs, col_piece, 2 * D), jnp.bfloat16
    )
    biases = score_biases(bias_table)

    def mix_specs(layer):
        stacks = (conv_weight, up_weight, down_weight)
        return [whole(norm_gain.shape)] + [layer_of(stack, layer) for stack in stacks]

    def attention_specs(layer):
        return [layer_of(stack, layer) for stack in (qkv_weight, proj_weight, biases)]

    after, normed_two = pl.pallas_call(
        regular_kernel,
        out_shape=(shape32, shape16),
        grid=(height // WS,),
        in_specs=[stripe(width), whole(norm_gain.shape)] + attention_specs(0),
        out_specs=(stripe(width), stripe(width)),
        name="regular_attention",
    )(tokens, norm_gain, qkv_weight, proj_weight, biases)

    current, received = pl.pallas_call(
        first_mix_kernel,
        out_shape=(shape16, moved),
        grid=(height // WS,),
        in_specs=[whole(blocked), stripe(width)] + mix_specs(0),
        out_specs=(stripe(width), pl.BlockSpec(memory_space=pl.ANY)),
        scratch_shapes=mix_scratch(height, width)
        + [
            pltpu.VMEM(
                (row_repeat * row_count, col_count, pairs, col_piece, 2 * D), jnp.bfloat16
            ),
            dma((row_repeat * row_count, col_count)),
            dma((row_count, col_count, row_repeat)),
        ],
        compiler_params=pltpu.CompilerParams(collective_id=0, has_side_effects=True),
        name="first_mix",
    )(
        normed_two.reshape(blocked),
        after,
        norm_gain,
        conv_weight,
        up_weight,
        down_weight,
    )

    returned = pl.pallas_call(
        shuffle_kernel,
        out_shape=moved,
        grid=(pairs,),
        in_specs=[
            pl.BlockSpec(
                (row_count, col_count, row_repeat, 1, col_piece, 2 * D),
                lambda i: (0, 0, 0, i, 0, 0),
            )
        ]
        + attention_specs(1),
        out_specs=pl.BlockSpec(memory_space=pl.ANY),
        scratch_shapes=[
            pltpu.VMEM(
                (pairs, row_count, col_count, row_repeat, col_piece, 2 * D), jnp.bfloat16
            ),
            dma((pairs, row_count, col_count)),
            dma((pairs, row_count, col_count)),
        ],
        compiler_params=pltpu.CompilerParams(collective_id=1, has_side_effects=True),
        name="shuffle_attention",
    )(received, qkv_weight, proj_weight, biases)

    return pl.pallas_call(
        last_mix_kernel,
        out_shape=shape16,
        grid=(height // WS,),
        in_specs=[whole(tokens.shape), whole(moved.shape)] + mix_specs(1),
        out_specs=stripe(width),
        scratch_shapes=[
            pltpu.VMEM(tokens.shape, jnp.float32),
            pltpu.VMEM(blocked, jnp.bfloat16),
        ]
        + mix_scratch(height, width),
        compiler_params=pltpu.CompilerParams(collective_id=2, has_side_effects=True),
        name="last_mix",
    )(current, returned, norm_gain, conv_weight, up_weight, down_weight)


def solution(mesh):
    in_specs = (P("row", "col", None), P(), P(), P(), P(), P(), P(), P())
    return jax.shard_map(
        on_device, mesh=mesh, in_specs=in_specs, out_specs=P("row", "col", None), check_vma=False
    )
```

```python
import functools

import jax
import jax.numpy as jnp
from jax import lax
from jax.experimental import pallas as pl
from jax.experimental.pallas import tpu as pltpu
from jax.sharding import PartitionSpec as P

D = 192
HEADS = 6
WS = 8
KS = 7
LAYERS = 2
HEAD = 32
AREA = WS * WS
HALO = KS // 2
LANES = 128

epsilon = 1e-05
LOG2E = 1.4426950408889634
VALUE_SCALE = 2.0**-8
EXP_CAP = 3.3895313892515355e38
MESH = pl.DeviceIdType.MESH
SIDES = [(d, a) for d in (-1, 0, 1) for a in (-1, 0, 1) if d or a]


def norm(values, gain):
    centre = jnp.mean(values, axis=-1, keepdims=True)
    centred = values - centre
    spread = jnp.mean(centred * centred, axis=-1, keepdims=True)
    return centred * lax.rsqrt(spread + epsilon) * gain


def score_biases(lookup_tables):
    places = jnp.arange(AREA, dtype=jnp.int32)
    row, col = places // WS, places % WS
    offsets = (row[:, None] - row[None, :] + WS - 1) * (2 * WS - 1) + (
        col[:, None] - col[None, :] + WS - 1
    )
    entries = jnp.arange((2 * WS - 1) * (2 * WS - 1), dtype=jnp.int32)
    selector = (offsets.reshape(-1)[None, :] == entries[:, None]).astype(jnp.float32)
    tables = lookup_tables.reshape(LAYERS * HEADS, -1)
    expanded = jnp.dot(tables, selector, precision=lax.Precision.HIGHEST) * LOG2E
    expanded = expanded.reshape(LAYERS, HEADS, AREA, AREA).transpose(0, 2, 1, 3)
    return expanded.reshape(LAYERS, AREA, HEADS * AREA)


def attention(normed, qkv_ref, proj_ref, bias_ref):
    count = normed.shape[0] // AREA
    query, key, value = (
        jnp.dot(
            normed, qkv_ref[:, part * D : (part + 1) * D], preferred_element_type=jnp.float32
        ).astype(jnp.bfloat16)
        for part in range(3)
    )
    lane_head = lax.broadcasted_iota(jnp.int32, (1, D), 1) // HEAD
    masks = [(lane_head == head).astype(jnp.bfloat16) for head in range(HEADS)]
    value_masks = [mask * VALUE_SCALE for mask in masks]
    sums = jnp.concatenate([jnp.broadcast_to(mask, (AREA, D)) for mask in value_masks], axis=0)
    bias = bias_ref[...]
    outs, exps = [], []
    for window in range(count):
        rows = slice(window * AREA, (window + 1) * AREA)
        keys = jnp.concatenate([key[rows] * mask for mask in masks], axis=0)
        scores = lax.dot_general(
            query[rows], keys, (((1,), (1,)), ((), ())), preferred_element_type=jnp.float32
        )
        exped = jnp.minimum(jnp.exp2(scores * (HEAD**-0.5 * LOG2E) + bias), EXP_CAP)
        exped = exped.astype(jnp.bfloat16)
        values = jnp.concatenate([value[rows] * mask for mask in value_masks], axis=0)
        outs.append(jnp.dot(exped, values, preferred_element_type=jnp.float32))
        exps.append(exped)
    total = jnp.dot(jnp.concatenate(exps, axis=0), sums, preferred_element_type=jnp.float32)
    attended = (jnp.concatenate(outs, axis=0) / total).astype(jnp.bfloat16)
    branch = jnp.dot(attended, proj_ref[...], preferred_element_type=jnp.float32)
    return branch.astype(jnp.bfloat16).astype(jnp.float32)


def regular_kernel(x_ref, gain_ref, qkv_ref, proj_ref, bias_ref, after_ref, normed_ref):
    rows, width = x_ref.shape[0], x_ref.shape[1]
    current = x_ref[...].astype(jnp.float32)
    normed = norm(current.reshape(rows * width, D), gain_ref[0, 0:1])
    windows = normed.reshape(WS, width // WS, WS, D).transpose(1, 0, 2, 3).reshape(rows * width, D)
    branch = attention(windows.astype(jnp.bfloat16), qkv_ref, proj_ref, bias_ref)
    branch = branch.reshape(width // WS, WS, WS, D).transpose(1, 0, 2, 3).reshape(rows, width, D)
    after = current + branch
    after_ref[...] = after
    normed_ref[...] = norm(after, gain_ref[1, 0:1]).astype(jnp.bfloat16)


def greet(everyone):
    rows, cols = lax.axis_size("row"), lax.axis_size("col")
    my_row, my_col = lax.axis_index("row"), lax.axis_index("col")
    barrier = pltpu.get_barrier_semaphore()
    if everyone:

        @pl.loop(0, rows * cols)
        def _(device):
            row, col = device // cols, device % cols

            @pl.when((row != my_row) | (col != my_col))
            def _():
                pl.semaphore_signal(barrier, 1, device_id=(row, col), device_id_type=MESH)

        pl.semaphore_wait(barrier, rows * cols - 1)
    else:
        for down, across in SIDES:
            row, col = my_row + down, my_col + across
            inside = (row >= 0) & (row < rows) & (col >= 0) & (col < cols)

            @pl.when(inside)
            def _():
                pl.semaphore_signal(barrier, 1, device_id=(row, col), device_id_type=MESH)

        beside_rows = (my_row > 0).astype(jnp.int32) + (my_row < rows - 1).astype(jnp.int32)
        beside_cols = (my_col > 0).astype(jnp.int32) + (my_col < cols - 1).astype(jnp.int32)
        pl.semaphore_wait(barrier, (1 + beside_rows) * (1 + beside_cols) - 1)


def exchange(normed_ref, wide, beside, above, corner, send_sem, recv_sem):
    rows, cols = lax.axis_size("row"), lax.axis_size("col")
    my_row, my_col = lax.axis_index("row"), lax.axis_index("col")
    height, blocks = normed_ref.shape[0], normed_ref.shape[1]
    width = blocks * 8
    links = []
    for number, (down, across) in enumerate(SIDES):
        row, col = my_row + down, my_col + across
        there = (row >= 0) & (row < rows) & (col >= 0) & (col < cols)
        back_row, back_col = my_row - down, my_col - across
        here = (back_row >= 0) & (back_row < rows) & (back_col >= 0) & (back_col < cols)
        picked = {-1: slice(0, HALO), 0: slice(0, height), 1: slice(height - HALO, height)}[down]
        if across == 0:
            source, target = normed_ref.at[picked], above.at[(1 - down) // 2]
        else:
            block = 0 if across < 0 else blocks - 1
            source = normed_ref.at[picked, block]
            side = (1 - across) // 2
            target = beside.at[side] if down == 0 else corner.at[(1 - down) // 2, side]
        copy = pltpu.make_async_remote_copy(
            source,
            target,
            send_sem.at[number],
            recv_sem.at[number],
            device_id=(row, col),
            device_id_type=MESH,
        )
        links.append((down, across, there, here, copy))
        pl.when(there)(copy.start)

    @pl.loop(0, height)
    def _(r):
        wide[HALO + r, 8 : 8 + width, :] = normed_ref[r].astype(jnp.float32).reshape(width, D)

    for down, across, there, here, copy in links:
        rows_at = {1: slice(0, HALO), 0: slice(HALO, HALO + height), -1: slice(HALO + height, None)}
        cols_at = {1: slice(0, 8), 0: slice(8, 8 + width), -1: slice(8 + width, None)}
        at = (rows_at[down], cols_at[across])

        @pl.when(here)
        def _():
            copy.wait_recv()
            if across == 0:
                landed = above[(1 - down) // 2].astype(jnp.float32).reshape(HALO, width, D)
            elif down == 0:
                landed = beside[(1 - across) // 2].astype(jnp.float32)
            else:
                landed = corner[(1 - down) // 2, (1 - across) // 2].astype(jnp.float32)
            wide[at[0], at[1], :] = landed

        @pl.when(jnp.logical_not(here))
        def _():
            wide[at[0], at[1], :] = jnp.zeros_like(wide[at[0], at[1], :])

        pl.when(there)(copy.wait_send)


def shift(layer, wide, low, high, taps, taps_ref):
    width = low.shape[2]
    own = taps_ref[:, layer]
    upper = own[:, LANES:]
    taps[0] = jnp.broadcast_to(own[:, :LANES][:, None, :], taps.shape[1:])
    both = jnp.concatenate([upper, upper], axis=-1)
    taps[1] = jnp.broadcast_to(both[:, None, :], taps.shape[1:])

    @pl.loop(0, wide.shape[0])
    def _(r):
        for v in range(KS):
            start = 8 - HALO + v
            low[v, r] = wide[r, start : start + width, :LANES]
            left = wide[r, start : start + width // 2, LANES:]
            right = wide[r, start + width // 2 : start + width, LANES:]
            high[v, r] = jnp.concatenate([left, right], axis=-1)


def mix(base, after, low, high, taps, conv, gain, up_ref, down_ref):
    rows, width = after.shape[0], after.shape[1]

    def tapped(cells, weights, left):
        sums = None
        for v in range(KS):
            for u in range(KS):
                term = cells[v, pl.ds(base + u, rows), left : left + 8, :]
                term = term * weights[u * KS + v][None]
                sums = term if sums is None else sums + term
        return sums

    for left in range(0, width, 8):
        at = slice(left, left + 8)
        conv[:, at, :LANES] = after[:, at, :LANES] + tapped(low, taps.at[0], left)
    for left in range(0, width // 2, 8):
        sums = tapped(high, taps.at[1], left)
        for half in range(2):
            at = slice(left + half * (width // 2), left + half * (width // 2) + 8)
            part = sums[:, :, half * (D - LANES) : (half + 1) * (D - LANES)]
            conv[:, at, LANES:] = after[:, at, LANES:] + part

    flat = conv[...].reshape(rows * width, D)
    normed = norm(flat, gain).astype(jnp.bfloat16)
    up = jnp.dot(normed, up_ref[...], preferred_element_type=jnp.float32)
    hidden = (0.5 * up * (1.0 + lax.erf(up * 0.5**0.5))).astype(jnp.bfloat16)
    outcome = flat + lax.dot_general(
        hidden, down_ref[...], (((1,), (1,)), ((), ())), preferred_element_type=jnp.float32
    )
    return outcome.astype(jnp.bfloat16)


def stripe_at(step, count):
    return (step + lax.axis_index("row")) % count


def first_mix_kernel(
    normed_ref,
    after_ref,
    gain_ref,
    taps_ref,
    up_ref,
    down_ref,
    out_ref,
    received,
    wide,
    low,
    high,
    taps,
    conv,
    beside,
    above,
    corner,
    halo_send,
    halo_recv,
    outgoing,
    send_sem,
    recv_sem,
):
    rows, width = after_ref.shape[0], after_ref.shape[1]
    row_count, col_count, row_repeat, pairs, col_piece = received.shape[:5]
    per_step = rows // (2 * pairs)
    my_row, my_col = lax.axis_index("row"), lax.axis_index("col")
    step = pl.program_id(0)
    turned = stripe_at(step, pl.num_programs(0))

    @pl.when(step == 0)
    def _():
        greet(True)
        exchange(normed_ref, wide, beside, above, corner, halo_send, halo_recv)
        shift(0, wide, low, high, taps, taps_ref)

    gain = gain_ref[2, 0:1]
    current = mix(turned * rows, after_ref, low, high, taps, conv, gain, up_ref, down_ref)
    out_ref[...] = current.reshape(rows, width, D)
    following = norm(current.astype(jnp.float32), gain_ref[0, 1:2]).reshape(rows, width, D)

    for k in range(per_step):
        for pair in range(pairs):
            row = (k * pairs + pair) * 2
            packed = jnp.concatenate([following[row], following[row + 1]], axis=-1)
            for col in range(col_count):
                piece = packed[col * col_piece : (col + 1) * col_piece]
                outgoing[turned * per_step + k, col, pair] = piece.astype(jnp.bfloat16)

    def remote(chunk, col):
        return pltpu.make_async_remote_copy(
            outgoing.at[chunk, col],
            received.at[my_row, my_col, chunk // row_count],
            send_sem.at[chunk, col],
            recv_sem.at[my_row, my_col, chunk // row_count],
            device_id=(chunk % row_count, col),
            device_id_type=MESH,
        )

    @pl.loop(0, col_count)
    def _(turn):
        col = (my_col + turn) % col_count
        for k in range(per_step):
            chunk = turned * per_step + k
            mine = (chunk % row_count == my_row) & (col == my_col)

            @pl.when(mine)
            def _():
                pltpu.make_async_copy(
                    outgoing.at[chunk, col],
                    received.at[my_row, my_col, chunk // row_count],
                    recv_sem.at[my_row, my_col, chunk // row_count],
                ).start()

            @pl.when(jnp.logical_not(mine))
            def _():
                remote(chunk, col).start()

    @pl.when(step == pl.num_programs(0) - 1)
    def _():
        @pl.loop(0, row_count * row_repeat)
        def _(chunk):
            @pl.loop(0, col_count)
            def _(col):
                mine = (chunk % row_count == my_row) & (col == my_col)

                @pl.when(jnp.logical_not(mine))
                def _():
                    remote(chunk, col).wait_send()

                row, repeat = chunk % row_count, chunk // row_count
                pltpu.make_async_copy(
                    outgoing.at[chunk, col],
                    received.at[row, col, repeat],
                    recv_sem.at[row, col, repeat],
                ).wait()


def shuffle_kernel(
    x_ref, qkv_ref, proj_ref, bias_ref, returned, outgoing, send_sem, recv_sem
):
    row_count, col_count, row_repeat, pairs, col_piece = returned.shape[:5]
    per_b = col_count // WS
    across = per_b * col_piece
    my_row, my_col = lax.axis_index("row"), lax.axis_index("col")
    step = pl.program_id(0)

    @pl.when(step == 0)
    def _():
        greet(True)

    tokens = x_ref[:, :, :, 0].astype(jnp.float32).transpose(0, 2, 1, 3, 4)
    tokens = tokens.reshape(WS, WS, per_b, col_piece, 2 * D)
    if per_b == 1:
        tokens = tokens[:, :, 0]
    else:
        tokens = jnp.concatenate([tokens[:, :, part] for part in range(per_b)], axis=2)
    results = []
    for half in range(2):
        windows = jnp.swapaxes(tokens[..., half * D : (half + 1) * D], 1, 2)
        windows = windows.transpose(1, 0, 2, 3).reshape(across * AREA, D)
        branch = attention(windows.astype(jnp.bfloat16), qkv_ref, proj_ref, bias_ref)
        branch = branch.reshape(across, WS, WS, D).transpose(1, 0, 2, 3)
        results.append(jnp.swapaxes(branch, 1, 2))
    packed = jnp.concatenate(results, axis=-1).reshape(row_count, row_repeat, WS, across, 2 * D)
    for col in range(col_count):
        part = col % per_b
        piece = packed[:, :, col // per_b, part * col_piece : (part + 1) * col_piece]
        outgoing[step, :, col] = piece.astype(jnp.bfloat16)

    def remote(pair, row, col):
        return pltpu.make_async_remote_copy(
            outgoing.at[pair, row, col],
            returned.at[my_row, my_col, :, pair],
            send_sem.at[pair, row, col],
            recv_sem.at[pair, my_row, my_col],
            device_id=(row, col),
            device_id_type=MESH,
        )

    def local(pair, row, col):
        return pltpu.make_async_copy(
            outgoing.at[pair, row, col],
            returned.at[row, col, :, pair],
            recv_sem.at[pair, row, col],
        )

    @pl.loop(0, col_count)
    def _(turn):
        col = (my_col + turn) % col_count

        @pl.loop(0, row_count)
        def _(row_turn):
            row = (my_row + row_turn) % row_count
            mine = (row == my_row) & (col == my_col)
            pl.when(mine)(lambda: local(step, row, col).start())
            pl.when(jnp.logical_not(mine))(lambda: remote(step, row, col).start())

    @pl.when(step == pl.num_programs(0) - 1)
    def _():
        @pl.loop(0, row_count * pairs)
        def _(both):
            pair, row = both // row_count, both % row_count

            @pl.loop(0, col_count)
            def _(col):
                mine = (row == my_row) & (col == my_col)
                pl.when(jnp.logical_not(mine))(lambda: remote(pair, row, col).wait_send())
                local(pair, row, col).wait()


def last_mix_kernel(
    current_ref,
    returned_ref,
    gain_ref,
    taps_ref,
    up_ref,
    down_ref,
    out_ref,
    after,
    normed,
    wide,
    low,
    high,
    taps,
    conv,
    beside,
    above,
    corner,
    halo_send,
    halo_recv,
):
    rows, width = out_ref.shape[0], out_ref.shape[1]
    row_count, col_count, row_repeat, pairs, col_piece = returned_ref.shape[:5]
    step = pl.program_id(0)

    @pl.when(step == 0)
    def _():

        @pl.loop(0, row_count * row_repeat)
        def _(chunk):
            for pair in range(pairs):
                packed = returned_ref[chunk % row_count, :, chunk // row_count, pair]
                packed = packed.astype(jnp.float32).reshape(width, 2 * D)
                for half in range(2):
                    row = (chunk * pairs + pair) * 2 + half
                    total = current_ref[row].astype(jnp.float32)
                    total = total + packed[:, half * D : (half + 1) * D]
                    after[row] = total
                    normed[row] = (
                        norm(total, gain_ref[1, 1:2]).reshape(width // 8, 8, D).astype(jnp.bfloat16)
                    )

        greet(False)
        exchange(normed, wide, beside, above, corner, halo_send, halo_recv)
        shift(1, wide, low, high, taps, taps_ref)

    base = step * rows
    gain = gain_ref[2, 1:2]
    stripes = after.at[pl.ds(base, rows)]
    current = mix(base, stripes, low, high, taps, conv, gain, up_ref, down_ref)
    out_ref[...] = current.reshape(rows, width, D)


def whole(shape):
    return pl.BlockSpec(shape, lambda i: (0,) * len(shape))


def layer_of(array, layer):
    block = (None,) + array.shape[1:]
    return pl.BlockSpec(block, lambda i: (layer,) + (0,) * (len(block) - 1))


def stripe(width):
    return pl.BlockSpec((WS, width, D), lambda i: (i, 0, 0))


def mix_scratch(height, width):
    dma = pltpu.SemaphoreType.DMA
    return [
        pltpu.VMEM((height + 2 * HALO, width + 16, D), jnp.float32),
        pltpu.VMEM((KS, height + 2 * HALO, width, LANES), jnp.float32),
        pltpu.VMEM((KS, height + 2 * HALO, width // 2, LANES), jnp.float32),
        pltpu.VMEM((2, KS * KS, 8, LANES), jnp.float32),
        pltpu.VMEM((WS, width, D), jnp.float32),
        pltpu.VMEM((2, height, 8, D), jnp.bfloat16),
        pltpu.VMEM((2, HALO, width // 8, 8, D), jnp.bfloat16),
        pltpu.VMEM((2, 2, HALO, 8, D), jnp.bfloat16),
        dma((len(SIDES),)),
        dma((len(SIDES),)),
    ]


def on_device(
    tokens, norm_gain, qkv_weight, proj_weight, bias_table, conv_weight, up_weight, down_weight
):
    height, width = tokens.shape[0], tokens.shape[1]
    row_count, col_count = lax.axis_size("row"), lax.axis_size("col")
    row_repeat = max(1, WS // row_count)
    row_piece = height // row_repeat // row_count
    col_piece = width // col_count
    pairs = row_piece // 2
    dma = pltpu.SemaphoreType.DMA
    shape32 = jax.ShapeDtypeStruct(tokens.shape, jnp.float32)
    shape16 = jax.ShapeDtypeStruct(tokens.shape, jnp.bfloat16)
    blocked = (height, width // 8, 8, D)
    moved = jax.ShapeDtypeStruct(
        (row_count, col_count, row_repeat, pairs, col_piece, 2 * D), jnp.bfloat16
    )
    biases = score_biases(bias_table)
    gains, taps = norm_gain.transpose(1, 0, 2), conv_weight.transpose(1, 0, 2)
    down_turned = down_weight.transpose(0, 2, 1)

    def mix_specs(layer):
        stacks = (up_weight, down_turned)
        return [whole(gains.shape), whole(taps.shape)] + [layer_of(x, layer) for x in stacks]

    def attention_specs(layer):
        return [layer_of(stack, layer) for stack in (qkv_weight, proj_weight, biases)]

    after, normed_two = pl.pallas_call(
        regular_kernel,
        out_shape=(shape32, shape16),
        grid=(height // WS,),
        in_specs=[stripe(width), whole(gains.shape)] + attention_specs(0),
        out_specs=(stripe(width), stripe(width)),
        name="regular_attention",
    )(tokens, gains, qkv_weight, proj_weight, biases)

    turned = pl.BlockSpec((WS, width, D), lambda i: (stripe_at(i, height // WS), 0, 0))
    current, received = pl.pallas_call(
        first_mix_kernel,
        out_shape=(shape16, moved),
        grid=(height // WS,),
        in_specs=[whole(blocked), turned] + mix_specs(0),
        out_specs=(turned, pl.BlockSpec(memory_space=pl.ANY)),
        scratch_shapes=mix_scratch(height, width)
        + [
            pltpu.VMEM(
                (row_repeat * row_count, col_count, pairs, col_piece, 2 * D), jnp.bfloat16
            ),
            dma((row_repeat * row_count, col_count)),
            dma((row_count, col_count, row_repeat)),
        ],
        compiler_params=pltpu.CompilerParams(collective_id=0, has_side_effects=True),
        name="first_mix",
    )(
        normed_two.reshape(blocked),
        after,
        gains,
        taps,
        up_weight,
        down_turned,
    )

    returned = pl.pallas_call(
        shuffle_kernel,
        out_shape=moved,
        grid=(pairs,),
        in_specs=[
            pl.BlockSpec(
                (row_count, col_count, row_repeat, 1, col_piece, 2 * D),
                lambda i: (0, 0, 0, i, 0, 0),
            )
        ]
        + attention_specs(1),
        out_specs=pl.BlockSpec(memory_space=pl.ANY),
        scratch_shapes=[
            pltpu.VMEM(
                (pairs, row_count, col_count, row_repeat, col_piece, 2 * D), jnp.bfloat16
            ),
            dma((pairs, row_count, col_count)),
            dma((pairs, row_count, col_count)),
        ],
        compiler_params=pltpu.CompilerParams(collective_id=1, has_side_effects=True),
        name="shuffle_attention",
    )(received, qkv_weight, proj_weight, biases)

    return pl.pallas_call(
        last_mix_kernel,
        out_shape=shape16,
        grid=(height // WS,),
        in_specs=[whole(tokens.shape), whole(moved.shape)] + mix_specs(1),
        out_specs=stripe(width),
        scratch_shapes=[
            pltpu.VMEM(tokens.shape, jnp.float32),
            pltpu.VMEM(blocked, jnp.bfloat16),
        ]
        + mix_scratch(height, width),
        compiler_params=pltpu.CompilerParams(collective_id=2, has_side_effects=True),
        name="last_mix",
    )(current, returned, gains, taps, up_weight, down_turned)


def solution(mesh):
    in_specs = (P("row", "col", None), P(), P(), P(), P(), P(), P(), P())
    return jax.shard_map(
        on_device, mesh=mesh, in_specs=in_specs, out_specs=P("row", "col", None), check_vma=False
    )
```

```python
import functools

import jax
import jax.numpy as jnp
from jax import lax
from jax.experimental import pallas as pl
from jax.experimental.pallas import tpu as pltpu
from jax.sharding import PartitionSpec as P

D = 192
HEADS = 6
WS = 8
KS = 7
LAYERS = 2
HEAD = 32
AREA = WS * WS
HALO = KS // 2
LANES = 128

epsilon = 1e-05
LOG2E = 1.4426950408889634
VALUE_SCALE = 2.0**-8
EXP_CAP = 3.3895313892515355e38
MESH = pl.DeviceIdType.MESH
SIDES = [(d, a) for d in (-1, 0, 1) for a in (-1, 0, 1) if d or a]


def norm(values, gain):
    centre = jnp.mean(values, axis=-1, keepdims=True)
    centred = values - centre
    spread = jnp.mean(centred * centred, axis=-1, keepdims=True)
    return centred * lax.rsqrt(spread + epsilon) * gain


def score_biases(lookup_tables):
    places = jnp.arange(AREA, dtype=jnp.int32)
    row, col = places // WS, places % WS
    offsets = (row[:, None] - row[None, :] + WS - 1) * (2 * WS - 1) + (
        col[:, None] - col[None, :] + WS - 1
    )
    entries = jnp.arange((2 * WS - 1) * (2 * WS - 1), dtype=jnp.int32)
    selector = (offsets.reshape(-1)[None, :] == entries[:, None]).astype(jnp.float32)
    tables = lookup_tables.reshape(LAYERS * HEADS, -1)
    expanded = jnp.dot(tables, selector, precision=lax.Precision.HIGHEST) * LOG2E
    expanded = expanded.reshape(LAYERS, HEADS, AREA, AREA).transpose(0, 2, 1, 3)
    return expanded.reshape(LAYERS, AREA, HEADS * AREA)


def attention(normed, qkv_ref, proj_ref, bias_ref):
    count = normed.shape[0] // AREA
    query, key, value = (
        jnp.dot(
            normed, qkv_ref[:, part * D : (part + 1) * D], preferred_element_type=jnp.float32
        ).astype(jnp.bfloat16)
        for part in range(3)
    )
    lane_head = lax.broadcasted_iota(jnp.int32, (1, D), 1) // HEAD
    masks = [(lane_head == head).astype(jnp.bfloat16) for head in range(HEADS)]
    value_masks = [mask * VALUE_SCALE for mask in masks]
    sums = jnp.concatenate([jnp.broadcast_to(mask, (AREA, D)) for mask in value_masks], axis=0)
    bias = bias_ref[...]
    outs, exps = [], []
    for window in range(count):
        rows = slice(window * AREA, (window + 1) * AREA)
        keys = jnp.concatenate([key[rows] * mask for mask in masks], axis=0)
        scores = lax.dot_general(
            query[rows], keys, (((1,), (1,)), ((), ())), preferred_element_type=jnp.float32
        )
        exped = jnp.minimum(jnp.exp2(scores * (HEAD**-0.5 * LOG2E) + bias), EXP_CAP)
        exped = exped.astype(jnp.bfloat16)
        values = jnp.concatenate([value[rows] * mask for mask in value_masks], axis=0)
        outs.append(jnp.dot(exped, values, preferred_element_type=jnp.float32))
        exps.append(exped)
    total = jnp.dot(jnp.concatenate(exps, axis=0), sums, preferred_element_type=jnp.float32)
    attended = (jnp.concatenate(outs, axis=0) / total).astype(jnp.bfloat16)
    branch = jnp.dot(attended, proj_ref[...], preferred_element_type=jnp.float32)
    return branch.astype(jnp.bfloat16).astype(jnp.float32)


def regular_kernel(x_ref, gain_ref, qkv_ref, proj_ref, bias_ref, after_ref, normed_ref):
    rows, width = x_ref.shape[0], x_ref.shape[1]
    current = x_ref[...].astype(jnp.float32)
    normed = norm(current.reshape(rows * width, D), gain_ref[0, 0:1])
    windows = normed.reshape(WS, width // WS, WS, D).transpose(1, 0, 2, 3).reshape(rows * width, D)
    branch = attention(windows.astype(jnp.bfloat16), qkv_ref, proj_ref, bias_ref)
    branch = branch.reshape(width // WS, WS, WS, D).transpose(1, 0, 2, 3).reshape(rows, width, D)
    after = current + branch
    after_ref[...] = after
    normed_ref[...] = norm(after, gain_ref[1, 0:1]).astype(jnp.bfloat16)


def greet(everyone):
    rows, cols = lax.axis_size("row"), lax.axis_size("col")
    my_row, my_col = lax.axis_index("row"), lax.axis_index("col")
    barrier = pltpu.get_barrier_semaphore()
    if everyone:

        @pl.loop(0, rows * cols)
        def _(device):
            row, col = device // cols, device % cols

            @pl.when((row != my_row) | (col != my_col))
            def _():
                pl.semaphore_signal(barrier, 1, device_id=(row, col), device_id_type=MESH)

        pl.semaphore_wait(barrier, rows * cols - 1)
    else:
        for down, across in SIDES:
            row, col = my_row + down, my_col + across
            inside = (row >= 0) & (row < rows) & (col >= 0) & (col < cols)

            @pl.when(inside)
            def _():
                pl.semaphore_signal(barrier, 1, device_id=(row, col), device_id_type=MESH)

        beside_rows = (my_row > 0).astype(jnp.int32) + (my_row < rows - 1).astype(jnp.int32)
        beside_cols = (my_col > 0).astype(jnp.int32) + (my_col < cols - 1).astype(jnp.int32)
        pl.semaphore_wait(barrier, (1 + beside_rows) * (1 + beside_cols) - 1)


def exchange(normed_ref, wide, beside, above, corner, send_sem, recv_sem):
    rows, cols = lax.axis_size("row"), lax.axis_size("col")
    my_row, my_col = lax.axis_index("row"), lax.axis_index("col")
    height, blocks = normed_ref.shape[0], normed_ref.shape[1]
    width = blocks * 8
    links = []
    for number, (down, across) in enumerate(SIDES):
        row, col = my_row + down, my_col + across
        there = (row >= 0) & (row < rows) & (col >= 0) & (col < cols)
        back_row, back_col = my_row - down, my_col - across
        here = (back_row >= 0) & (back_row < rows) & (back_col >= 0) & (back_col < cols)
        picked = {-1: slice(0, HALO), 0: slice(0, height), 1: slice(height - HALO, height)}[down]
        if across == 0:
            source, target = normed_ref.at[picked], above.at[(1 - down) // 2]
        else:
            block = 0 if across < 0 else blocks - 1
            source = normed_ref.at[picked, block]
            side = (1 - across) // 2
            target = beside.at[side] if down == 0 else corner.at[(1 - down) // 2, side]
        copy = pltpu.make_async_remote_copy(
            source,
            target,
            send_sem.at[number],
            recv_sem.at[number],
            device_id=(row, col),
            device_id_type=MESH,
        )
        links.append((down, across, there, here, copy))
        pl.when(there)(copy.start)

    @pl.loop(0, height)
    def _(r):
        wide[HALO + r, 8 : 8 + width, :] = normed_ref[r].astype(jnp.float32).reshape(width, D)

    for down, across, there, here, copy in links:
        rows_at = {1: slice(0, HALO), 0: slice(HALO, HALO + height), -1: slice(HALO + height, None)}
        cols_at = {1: slice(0, 8), 0: slice(8, 8 + width), -1: slice(8 + width, None)}
        at = (rows_at[down], cols_at[across])

        @pl.when(here)
        def _():
            copy.wait_recv()
            if across == 0:
                landed = above[(1 - down) // 2].astype(jnp.float32).reshape(HALO, width, D)
            elif down == 0:
                landed = beside[(1 - across) // 2].astype(jnp.float32)
            else:
                landed = corner[(1 - down) // 2, (1 - across) // 2].astype(jnp.float32)
            wide[at[0], at[1], :] = landed

        @pl.when(jnp.logical_not(here))
        def _():
            wide[at[0], at[1], :] = jnp.zeros_like(wide[at[0], at[1], :])

        pl.when(there)(copy.wait_send)


def shift(layer, wide, low, high, taps, taps_ref):
    width = low.shape[2]
    own = taps_ref[:, layer]
    upper = own[:, LANES:]
    taps[0] = jnp.broadcast_to(own[:, :LANES][:, None, :], taps.shape[1:])
    both = jnp.concatenate([upper, upper], axis=-1)
    taps[1] = jnp.broadcast_to(both[:, None, :], taps.shape[1:])

    @pl.loop(0, wide.shape[0])
    def _(r):
        for v in range(KS):
            start = 8 - HALO + v
            low[v, r] = wide[r, start : start + width, :LANES]
            left = wide[r, start : start + width // 2, LANES:]
            right = wide[r, start + width // 2 : start + width, LANES:]
            high[v, r] = jnp.concatenate([left, right], axis=-1)


def mix(base, after, low, high, taps, conv, gain, up_ref, down_ref):
    rows, width = after.shape[0], after.shape[1]

    def tapped(cells, weights, left):
        sums = None
        for v in range(KS):
            for u in range(KS):
                term = cells[v, pl.ds(base + u, rows), left : left + 8, :]
                term = term * weights[u * KS + v][None]
                sums = term if sums is None else sums + term
        return sums

    for left in range(0, width, 8):
        at = slice(left, left + 8)
        conv[:, at, :LANES] = after[:, at, :LANES] + tapped(low, taps.at[0], left)
    for left in range(0, width // 2, 8):
        sums = tapped(high, taps.at[1], left)
        for half in range(2):
            at = slice(left + half * (width // 2), left + half * (width // 2) + 8)
            part = sums[:, :, half * (D - LANES) : (half + 1) * (D - LANES)]
            conv[:, at, LANES:] = after[:, at, LANES:] + part

    flat = conv[...].reshape(rows * width, D)
    normed = norm(flat, gain).astype(jnp.bfloat16)
    up = jnp.dot(normed, up_ref[...], preferred_element_type=jnp.float32)
    hidden = (0.5 * up * (1.0 + lax.erf(up * 0.5**0.5))).astype(jnp.bfloat16)
    outcome = flat + lax.dot_general(
        hidden, down_ref[...], (((1,), (1,)), ((), ())), preferred_element_type=jnp.float32
    )
    return outcome.astype(jnp.bfloat16)


def stripe_at(step, count):
    return (step + lax.axis_index("row")) % count


def first_mix_kernel(
    normed_ref,
    after_ref,
    gain_ref,
    taps_ref,
    up_ref,
    down_ref,
    out_ref,
    received,
    wide,
    low,
    high,
    taps,
    conv,
    beside,
    above,
    corner,
    halo_send,
    halo_recv,
    outgoing,
    send_sem,
    recv_sem,
):
    rows, width = after_ref.shape[0], after_ref.shape[1]
    row_count, col_count, row_repeat, pairs, col_piece = received.shape[:5]
    per_step = rows // (2 * pairs)
    my_row, my_col = lax.axis_index("row"), lax.axis_index("col")
    step = pl.program_id(0)
    turned = stripe_at(step, pl.num_programs(0))

    @pl.when(step == 0)
    def _():
        greet(True)
        exchange(normed_ref, wide, beside, above, corner, halo_send, halo_recv)
        shift(0, wide, low, high, taps, taps_ref)

    gain = gain_ref[2, 0:1]
    current = mix(turned * rows, after_ref, low, high, taps, conv, gain, up_ref, down_ref)
    out_ref[...] = current.reshape(rows, width, D)
    following = norm(current.astype(jnp.float32), gain_ref[0, 1:2]).reshape(rows, width, D)

    for k in range(per_step):
        for pair in range(pairs):
            row = (k * pairs + pair) * 2
            packed = jnp.concatenate([following[row], following[row + 1]], axis=-1)
            for col in range(col_count):
                piece = packed[col * col_piece : (col + 1) * col_piece]
                outgoing[turned * per_step + k, col, pair] = piece.astype(jnp.bfloat16)

    def remote(chunk, col):
        return pltpu.make_async_remote_copy(
            outgoing.at[chunk, col],
            received.at[my_row, my_col, chunk // row_count],
            send_sem.at[chunk, col],
            recv_sem.at[my_row, my_col, chunk // row_count],
            device_id=(chunk % row_count, col),
            device_id_type=MESH,
        )

    @pl.loop(0, col_count)
    def _(turn):
        col = (my_col + col_count // 2 + turn) % col_count
        for k in range(per_step):
            chunk = turned * per_step + k
            mine = (chunk % row_count == my_row) & (col == my_col)

            @pl.when(mine)
            def _():
                pltpu.make_async_copy(
                    outgoing.at[chunk, col],
                    received.at[my_row, my_col, chunk // row_count],
                    recv_sem.at[my_row, my_col, chunk // row_count],
                ).start()

            @pl.when(jnp.logical_not(mine))
            def _():
                remote(chunk, col).start()

    @pl.when(step == pl.num_programs(0) - 1)
    def _():
        @pl.loop(0, row_count * row_repeat)
        def _(chunk):
            @pl.loop(0, col_count)
            def _(col):
                mine = (chunk % row_count == my_row) & (col == my_col)

                @pl.when(jnp.logical_not(mine))
                def _():
                    remote(chunk, col).wait_send()

                row, repeat = chunk % row_count, chunk // row_count
                pltpu.make_async_copy(
                    outgoing.at[chunk, col],
                    received.at[row, col, repeat],
                    recv_sem.at[row, col, repeat],
                ).wait()


def shuffle_kernel(
    x_ref, qkv_ref, proj_ref, bias_ref, returned, outgoing, send_sem, recv_sem
):
    row_count, col_count, row_repeat, pairs, col_piece = returned.shape[:5]
    per_b = col_count // WS
    across = per_b * col_piece
    my_row, my_col = lax.axis_index("row"), lax.axis_index("col")
    step = pl.program_id(0)

    @pl.when(step == 0)
    def _():
        greet(True)

    tokens = x_ref[:, :, :, 0].astype(jnp.float32).transpose(0, 2, 1, 3, 4)
    tokens = tokens.reshape(WS, WS, per_b, col_piece, 2 * D)
    if per_b == 1:
        tokens = tokens[:, :, 0]
    else:
        tokens = jnp.concatenate([tokens[:, :, part] for part in range(per_b)], axis=2)
    results = []
    for half in range(2):
        windows = jnp.swapaxes(tokens[..., half * D : (half + 1) * D], 1, 2)
        windows = windows.transpose(1, 0, 2, 3).reshape(across * AREA, D)
        branch = attention(windows.astype(jnp.bfloat16), qkv_ref, proj_ref, bias_ref)
        branch = branch.reshape(across, WS, WS, D).transpose(1, 0, 2, 3)
        results.append(jnp.swapaxes(branch, 1, 2))
    packed = jnp.concatenate(results, axis=-1).reshape(row_count, row_repeat, WS, across, 2 * D)
    for col in range(col_count):
        part = col % per_b
        piece = packed[:, :, col // per_b, part * col_piece : (part + 1) * col_piece]
        outgoing[step, :, col] = piece.astype(jnp.bfloat16)

    def remote(pair, row, col):
        return pltpu.make_async_remote_copy(
            outgoing.at[pair, row, col],
            returned.at[my_row, my_col, :, pair],
            send_sem.at[pair, row, col],
            recv_sem.at[pair, my_row, my_col],
            device_id=(row, col),
            device_id_type=MESH,
        )

    def local(pair, row, col):
        return pltpu.make_async_copy(
            outgoing.at[pair, row, col],
            returned.at[row, col, :, pair],
            recv_sem.at[pair, row, col],
        )

    @pl.loop(0, col_count)
    def _(turn):
        col = (my_col + col_count // 2 + turn) % col_count

        @pl.loop(0, row_count)
        def _(row_turn):
            row = (my_row + row_turn) % row_count
            mine = (row == my_row) & (col == my_col)
            pl.when(mine)(lambda: local(step, row, col).start())
            pl.when(jnp.logical_not(mine))(lambda: remote(step, row, col).start())

    @pl.when(step == pl.num_programs(0) - 1)
    def _():
        @pl.loop(0, row_count * pairs)
        def _(both):
            pair, row = both // row_count, both % row_count

            @pl.loop(0, col_count)
            def _(col):
                mine = (row == my_row) & (col == my_col)
                pl.when(jnp.logical_not(mine))(lambda: remote(pair, row, col).wait_send())
                local(pair, row, col).wait()


def last_mix_kernel(
    current_ref,
    returned_ref,
    gain_ref,
    taps_ref,
    up_ref,
    down_ref,
    out_ref,
    after,
    normed,
    wide,
    low,
    high,
    taps,
    conv,
    beside,
    above,
    corner,
    halo_send,
    halo_recv,
):
    rows, width = out_ref.shape[0], out_ref.shape[1]
    row_count, col_count, row_repeat, pairs, col_piece = returned_ref.shape[:5]
    step = pl.program_id(0)

    @pl.when(step == 0)
    def _():

        @pl.loop(0, row_count * row_repeat)
        def _(chunk):
            for pair in range(pairs):
                packed = returned_ref[chunk % row_count, :, chunk // row_count, pair]
                packed = packed.astype(jnp.float32).reshape(width, 2 * D)
                for half in range(2):
                    row = (chunk * pairs + pair) * 2 + half
                    total = current_ref[row].astype(jnp.float32)
                    total = total + packed[:, half * D : (half + 1) * D]
                    after[row] = total
                    normed[row] = (
                        norm(total, gain_ref[1, 1:2]).reshape(width // 8, 8, D).astype(jnp.bfloat16)
                    )

        greet(False)
        exchange(normed, wide, beside, above, corner, halo_send, halo_recv)
        shift(1, wide, low, high, taps, taps_ref)

    base = step * rows
    gain = gain_ref[2, 1:2]
    stripes = after.at[pl.ds(base, rows)]
    current = mix(base, stripes, low, high, taps, conv, gain, up_ref, down_ref)
    out_ref[...] = current.reshape(rows, width, D)


def whole(shape):
    return pl.BlockSpec(shape, lambda i: (0,) * len(shape))


def layer_of(array, layer):
    block = (None,) + array.shape[1:]
    return pl.BlockSpec(block, lambda i: (layer,) + (0,) * (len(block) - 1))


def stripe(width):
    return pl.BlockSpec((WS, width, D), lambda i: (i, 0, 0))


def mix_scratch(height, width):
    dma = pltpu.SemaphoreType.DMA
    return [
        pltpu.VMEM((height + 2 * HALO, width + 16, D), jnp.float32),
        pltpu.VMEM((KS, height + 2 * HALO, width, LANES), jnp.float32),
        pltpu.VMEM((KS, height + 2 * HALO, width // 2, LANES), jnp.float32),
        pltpu.VMEM((2, KS * KS, 8, LANES), jnp.float32),
        pltpu.VMEM((WS, width, D), jnp.float32),
        pltpu.VMEM((2, height, 8, D), jnp.bfloat16),
        pltpu.VMEM((2, HALO, width // 8, 8, D), jnp.bfloat16),
        pltpu.VMEM((2, 2, HALO, 8, D), jnp.bfloat16),
        dma((len(SIDES),)),
        dma((len(SIDES),)),
    ]


def on_device(
    tokens, norm_gain, qkv_weight, proj_weight, bias_table, conv_weight, up_weight, down_weight
):
    height, width = tokens.shape[0], tokens.shape[1]
    row_count, col_count = lax.axis_size("row"), lax.axis_size("col")
    row_repeat = max(1, WS // row_count)
    row_piece = height // row_repeat // row_count
    col_piece = width // col_count
    pairs = row_piece // 2
    dma = pltpu.SemaphoreType.DMA
    shape32 = jax.ShapeDtypeStruct(tokens.shape, jnp.float32)
    shape16 = jax.ShapeDtypeStruct(tokens.shape, jnp.bfloat16)
    blocked = (height, width // 8, 8, D)
    moved = jax.ShapeDtypeStruct(
        (row_count, col_count, row_repeat, pairs, col_piece, 2 * D), jnp.bfloat16
    )
    biases = score_biases(bias_table)
    gains, taps = norm_gain.transpose(1, 0, 2), conv_weight.transpose(1, 0, 2)
    down_turned = down_weight.transpose(0, 2, 1)

    def mix_specs(layer):
        stacks = (up_weight, down_turned)
        return [whole(gains.shape), whole(taps.shape)] + [layer_of(x, layer) for x in stacks]

    def attention_specs(layer):
        return [layer_of(stack, layer) for stack in (qkv_weight, proj_weight, biases)]

    after, normed_two = pl.pallas_call(
        regular_kernel,
        out_shape=(shape32, shape16),
        grid=(height // WS,),
        in_specs=[stripe(width), whole(gains.shape)] + attention_specs(0),
        out_specs=(stripe(width), stripe(width)),
        name="regular_attention",
    )(tokens, gains, qkv_weight, proj_weight, biases)

    turned = pl.BlockSpec((WS, width, D), lambda i: (stripe_at(i, height // WS), 0, 0))
    current, received = pl.pallas_call(
        first_mix_kernel,
        out_shape=(shape16, moved),
        grid=(height // WS,),
        in_specs=[whole(blocked), turned] + mix_specs(0),
        out_specs=(turned, pl.BlockSpec(memory_space=pl.ANY)),
        scratch_shapes=mix_scratch(height, width)
        + [
            pltpu.VMEM(
                (row_repeat * row_count, col_count, pairs, col_piece, 2 * D), jnp.bfloat16
            ),
            dma((row_repeat * row_count, col_count)),
            dma((row_count, col_count, row_repeat)),
        ],
        compiler_params=pltpu.CompilerParams(collective_id=0, has_side_effects=True),
        name="first_mix",
    )(
        normed_two.reshape(blocked),
        after,
        gains,
        taps,
        up_weight,
        down_turned,
    )

    returned = pl.pallas_call(
        shuffle_kernel,
        out_shape=moved,
        grid=(pairs,),
        in_specs=[
            pl.BlockSpec(
                (row_count, col_count, row_repeat, 1, col_piece, 2 * D),
                lambda i: (0, 0, 0, i, 0, 0),
            )
        ]
        + attention_specs(1),
        out_specs=pl.BlockSpec(memory_space=pl.ANY),
        scratch_shapes=[
            pltpu.VMEM(
                (pairs, row_count, col_count, row_repeat, col_piece, 2 * D), jnp.bfloat16
            ),
            dma((pairs, row_count, col_count)),
            dma((pairs, row_count, col_count)),
        ],
        compiler_params=pltpu.CompilerParams(collective_id=1, has_side_effects=True),
        name="shuffle_attention",
    )(received, qkv_weight, proj_weight, biases)

    return pl.pallas_call(
        last_mix_kernel,
        out_shape=shape16,
        grid=(height // WS,),
        in_specs=[whole(tokens.shape), whole(moved.shape)] + mix_specs(1),
        out_specs=stripe(width),
        scratch_shapes=[
            pltpu.VMEM(tokens.shape, jnp.float32),
            pltpu.VMEM(blocked, jnp.bfloat16),
        ]
        + mix_scratch(height, width),
        compiler_params=pltpu.CompilerParams(collective_id=2, has_side_effects=True),
        name="last_mix",
    )(current, returned, gains, taps, up_weight, down_turned)


def solution(mesh):
    in_specs = (P("row", "col", None), P(), P(), P(), P(), P(), P(), P())
    return jax.shard_map(
        on_device, mesh=mesh, in_specs=in_specs, out_specs=P("row", "col", None), check_vma=False
    )
```
